32 devices in a mesh: dp: 2 (over core), seq: 4 (over z), head: 4 (over y, x).
Axes of the slice: x: 2, y: 2, z: 4, core: 2. Of those that a mesh axis runs over, the one named last changes fastest.
Arguments:
- x_in: float32 [2, 512, 1024], P('dp', 'seq'), may hold values from -6 to 6
- cotangent: float32 [2, 512, 1024], P('dp', 'seq'), may hold values from -6 to 6
- attn_gain: bfloat16 [1024], P('seq'), may hold values from 0.25 to 1.75
- w_query: bfloat16 [1024, 512], P('seq', 'head'), may hold values from -0.1875 to 0.1875
- w_key: bfloat16 [1024, 512], P('seq', 'head'), may hold values from -0.1875 to 0.1875
- w_value: bfloat16 [1024, 1024], P('seq', 'head'), may hold values from -0.1875 to 0.1875
- w_outgate: bfloat16 [1024, 1024], P('seq', 'head'), may hold values from -0.1875 to 0.1875
- w_lowrank: bfloat16 [1024, 16], P('seq'), may hold values from -0.1875 to 0.1875
- w_forget: float32 [16, 512], replicated, may hold values from -1.5 to 1.5
- forget_bias: float32 [512], replicated, may hold values from -1 to 6
- group_gain: float32 [256], replicated, may hold values from 0.25 to 1.75
- w_output: bfloat16 [1024, 1024], P('head', 'seq'), may hold values from -0.375 to 0.375
- mlp_gain: bfloat16 [1024], P('seq'), may hold values from 0.25 to 1.75
- w_gate: bfloat16 [1024, 2816], P('seq', 'head'), may hold values from -0.1875 to 0.1875
- w_up: bfloat16 [1024, 2816], P('seq', 'head'), may hold values from -0.1875 to 0.1875
- w_down: bfloat16 [2816, 1024], P('head', 'seq'), may hold values from -0.109375 to 0.109375
Outputs:
- block_out: float32 [2, 512, 1024], P('dp', 'seq')
- grad_input: float32 [2, 512, 1024], P('dp', 'seq')
- grad_attn_gain: float32 [1024], P('seq')
- grad_query: float32 [1024, 512], P('seq', 'head')
- grad_key: float32 [1024, 512], P('seq', 'head')
- grad_value: float32 [1024, 1024], P('seq', 'head')
- grad_outgate: float32 [1024, 1024], P('seq', 'head')
- grad_lowrank: float32 [1024, 16], P('seq')
- grad_forget: float32 [16, 512], replicated
- grad_bias: float32 [512], replicated
- grad_group_gain: float32 [256], replicated
- grad_output: float32 [1024, 1024], P('head', 'seq')
- grad_mlp_gain: float32 [1024], P('seq')
- grad_gate: float32 [1024, 2816], P('seq', 'head')
- grad_up: float32 [1024, 2816], P('seq', 'head')
- grad_down: float32 [2816, 1024], P('head', 'seq')
The draws below stay inside these ranges and needn't reach their ends.
All inputs are finite; a program needn't handle non-finite values.
Results may differ from the reference program's by a relative error of at most 0.0097.
Values may be sent and summed in bfloat16 or wider, within the bound.
A program may use at most 128 MiB of HBM per device.

```python
import jax
import jax.numpy as jnp
from jax import lax

D = 1024
H = 4
DK = 128
DV = 256
R = 16
FF = 2816
SPAN = 64
LEN = 512
SEQS = 2


def shard_levels(stream_key, shape, split, low, high):
    def one(axis_at, blocks):
        draws = jax.random.uniform(jax.random.fold_in(jax.random.fold_in(stream_key, 6), axis_at), (blocks,), jnp.float32, low / len(split), high / len(split))
        return jnp.repeat(jnp.exp(draws), shape[axis_at] // blocks).reshape((-1,) + (1,) * (len(shape) - axis_at - 1))

    level = one(*split[0])
    for cut in split[1:]:
        level = level * one(*cut)
    return level


def normal_values(own_key, extent, width, most, shards=(), held_as=jnp.bfloat16):
    drawn = width * jax.random.normal(own_key, extent, jnp.float32)
    if shards:
        drawn = drawn * shard_levels(own_key, extent, shards, -0.22, 0.18)
    return jnp.clip(drawn, -most, most).astype(held_as)


def setup_inputs(seed: int = 0) -> dict:
    streams_of = jax.random.split(jax.random.key(seed), 17)
    x_in = normal_values(streams_of[0], (SEQS, LEN, D), 1.0, 6.0, ((0, 2), (1, 4)), jnp.float32)
    cotangent = normal_values(streams_of[1], (SEQS, LEN, D), 1.0, 6.0, ((0, 2), (1, 4)), jnp.float32)
    attn_gain = jnp.clip(1.0 + 0.15 * jax.random.normal(streams_of[2], (D,), jnp.float32), 0.25, 1.75).astype(jnp.bfloat16)
    w_query = normal_values(streams_of[3], (D, H * DK), D ** -0.5, 0.1875, ((0, 4), (1, 4)))
    w_key = normal_values(streams_of[4], (D, H * DK), D ** -0.5, 0.1875, ((0, 4), (1, 4)))
    w_value = normal_values(streams_of[5], (D, H * DV), D ** -0.5, 0.1875, ((0, 4), (1, 4)))
    w_outgate = normal_values(streams_of[6], (D, H * DV), D ** -0.5, 0.1875, ((0, 4), (1, 4)))
    w_lowrank = normal_values(streams_of[7], (D, R), D ** -0.5, 0.1875, ((0, 4),))
    w_forget = normal_values(streams_of[8], (R, H * DK), R ** -0.5, 1.5, (), jnp.float32)
    forget_bias = jnp.clip(jax.random.uniform(streams_of[9], (H * DK,), jnp.float32, -1.0, 6.0), -1.0, 6.0)
    group_gain = jnp.clip(1.0 + 0.15 * jax.random.normal(streams_of[10], (DV,), jnp.float32), 0.25, 1.75)
    w_output = normal_values(streams_of[11], (H * DV, D), DV ** -0.5, 0.375, ((0, 4), (1, 4)))
    mlp_gain = jnp.clip(1.0 + 0.15 * jax.random.normal(streams_of[12], (D,), jnp.float32), 0.25, 1.75).astype(jnp.bfloat16)
    w_gate = normal_values(streams_of[13], (D, FF), D ** -0.5, 0.1875, ((0, 4), (1, 4)))
    w_up = normal_values(streams_of[14], (D, FF), D ** -0.5, 0.1875, ((0, 4), (1, 4)))
    w_down = normal_values(streams_of[15], (FF, D), FF ** -0.5, 0.109375, ((0, 4), (1, 4)))
    return dict(x_in=x_in, cotangent=cotangent, attn_gain=attn_gain, w_query=w_query, w_key=w_key, w_value=w_value, w_outgate=w_outgate, w_lowrank=w_lowrank, w_forget=w_forget, forget_bias=forget_bias, group_gain=group_gain, w_output=w_output, mlp_gain=mlp_gain, w_gate=w_gate, w_up=w_up, w_down=w_down)


epsilon = 1e-06
normalizer = 16.0
highest = lax.Precision.HIGHEST

def product(left, right):
    return jnp.dot(left, right, preferred_element_type=jnp.float32)

def rms_rows(inputs):
    return lax.rsqrt(lax.optimization_barrier(jnp.mean(inputs * inputs, axis=-1, keepdims=True)) + epsilon)

def norm_back(inputs, scale, gain, grad):
    scaled = gain * grad
    gain_terms = grad * inputs * scale
    input_grad = scale * scaled - inputs * scale ** 3 * lax.optimization_barrier(jnp.mean(scaled * inputs, axis=-1, keepdims=True))
    return (gain_terms, input_grad)

def mixer_block(queries, keys_in, values_in, log_decay, start_state):
    blocks = queries.shape[0] // SPAN

    def cut(array):
        return array.reshape(blocks, SPAN, array.shape[-1])
    lower = jnp.tril(jnp.ones((SPAN, SPAN), jnp.float32))

    def block_step(carried, pieces):
        query_blk, key_blk, value_blk, decay_blk = pieces
        running = jnp.cumsum(decay_blk, axis=0)
        from_state = jnp.dot(query_blk * jnp.exp(running), carried, precision=highest)
        spread = jnp.exp(jnp.minimum(running[:, None, :] - running[None, :, :], 0.0)) * lower[:, :, None]
        scores = jnp.einsum('id,jd,ijd->ij', query_blk, key_blk, spread, precision=highest)
        inside = jnp.dot(scores, value_blk, precision=highest)
        ending = running[-1]
        weighted = key_blk * jnp.exp(ending[None, :] - running)
        carried = jnp.exp(ending)[:, None] * carried + jnp.dot(weighted.T, value_blk, precision=highest)
        return (carried, from_state + inside)
    final_state, outputs = lax.scan(jax.checkpoint(block_step), start_state, (cut(queries), cut(keys_in), cut(values_in), cut(log_decay)))
    return (outputs.reshape(queries.shape[0], values_in.shape[-1]), final_state)

def reference(x_in, cotangent, attn_gain, w_query, w_key, w_value, w_outgate, w_lowrank, w_forget, forget_bias, group_gain, w_output, mlp_gain, w_gate, w_up, w_down):
    head_scale = DK ** (-0.5)
    gain_first = attn_gain.astype(jnp.float32)
    gain_second = mlp_gain.astype(jnp.float32)

    def one_sequence(totals, pair):
        seq_in, seq_cot = pair
        length = seq_in.shape[0]

        def heads_of(array, size):
            return array.reshape(length, H, size).transpose(1, 0, 2)

        def rows_of(array):
            return array.transpose(1, 0, 2).reshape(length, -1)
        scale_one = rms_rows(seq_in)
        normed_in = (seq_in * scale_one * gain_first).astype(jnp.bfloat16)
        q_rows = product(normed_in, w_query)
        k_rows = product(normed_in, w_key)
        v_rows = product(normed_in, w_value)
        og_rows = product(normed_in, w_outgate)
        low_rank = product(normed_in, w_lowrank)
        pre_gate = jnp.dot(low_rank, w_forget, precision=highest) + forget_bias
        log_decay = jax.nn.log_sigmoid(pre_gate) / normalizer

        def mixed(q_heads, k_heads, v_heads, d_heads):
            zero_state = jnp.zeros((H, DK, DV), jnp.float32)
            return jax.vmap(mixer_block)(q_heads * head_scale, k_heads, v_heads, d_heads, zero_state)
        (o_heads, end_state), pullback = jax.vjp(mixed, heads_of(q_rows, DK), heads_of(k_rows, DK), heads_of(v_rows, DV), heads_of(log_decay, DK))
        gate_heads = heads_of(og_rows, DV)
        scale_three = rms_rows(o_heads)
        gated_norm = o_heads * scale_three * group_gain
        gate_sig = jax.nn.sigmoid(gate_heads)
        gate_act = gate_heads * gate_sig
        mixed_out = rows_of(gated_norm * gate_act).astype(jnp.bfloat16)
        resid = seq_in + product(mixed_out, w_output)
        scale_two = rms_rows(resid)
        normed_mid = (resid * scale_two * gain_second).astype(jnp.bfloat16)
        gate_pre = product(normed_mid, w_gate)
        up_pre = product(normed_mid, w_up)
        gate_sigma = jax.nn.sigmoid(gate_pre)
        gate_silu = gate_pre * gate_sigma
        mlp_hidden = (gate_silu * up_pre).astype(jnp.bfloat16)
        result = resid + product(mlp_hidden, w_down)
        grad_out_b = seq_cot.astype(jnp.bfloat16)
        d_down = product(mlp_hidden.T, grad_out_b)
        d_hidden = product(grad_out_b, w_down.T)
        d_gate_pre = (d_hidden * up_pre * gate_sigma * (1.0 + gate_pre * (1.0 - gate_sigma))).astype(jnp.bfloat16)
        d_up_pre = (d_hidden * gate_silu).astype(jnp.bfloat16)
        d_gate = product(normed_mid.T, d_gate_pre)
        d_up = product(normed_mid.T, d_up_pre)
        d_normed_mid = product(d_gate_pre, w_gate.T) + product(d_up_pre, w_up.T)
        gain_terms, d_resid_norm = norm_back(resid, scale_two, gain_second, d_normed_mid)
        d_gain_two = lax.optimization_barrier(jnp.sum(gain_terms, axis=0))
        d_resid = seq_cot + d_resid_norm
        d_resid_b = d_resid.astype(jnp.bfloat16)
        d_output = product(mixed_out.T, d_resid_b)
        d_mixed = heads_of(product(d_resid_b, w_output.T), DV)
        d_norm_out = d_mixed * gate_act
        d_gate_heads = d_mixed * gated_norm * gate_sig * (1.0 + gate_heads * (1.0 - gate_sig))
        d_group = lax.optimization_barrier(jnp.sum(d_norm_out * o_heads * scale_three, axis=(0, 1)))
        group_terms, d_o_heads = norm_back(o_heads, scale_three, group_gain, d_norm_out)
        d_q, d_k, d_v, d_decay = pullback((d_o_heads, jnp.zeros_like(end_state)))
        d_pre = rows_of(d_decay) / normalizer * jax.nn.sigmoid(-pre_gate)
        d_bias = lax.optimization_barrier(jnp.sum(d_pre, axis=0))
        d_forget = jnp.dot(low_rank.T, d_pre, precision=highest)
        d_low_b = jnp.dot(d_pre, w_forget.T, precision=highest).astype(jnp.bfloat16)
        d_q_b = rows_of(d_q).astype(jnp.bfloat16)
        d_k_b = rows_of(d_k).astype(jnp.bfloat16)
        d_v_b = rows_of(d_v).astype(jnp.bfloat16)
        d_og_b = rows_of(d_gate_heads).astype(jnp.bfloat16)
        d_query = product(normed_in.T, d_q_b)
        d_key = product(normed_in.T, d_k_b)
        d_value = product(normed_in.T, d_v_b)
        d_outgate = product(normed_in.T, d_og_b)
        d_lowrank = product(normed_in.T, d_low_b)
        d_normed_in = product(d_q_b, w_query.T) + product(d_k_b, w_key.T) + product(d_v_b, w_value.T) + product(d_og_b, w_outgate.T) + product(d_low_b, w_lowrank.T)
        first_terms, d_in_norm = norm_back(seq_in, scale_one, gain_first, d_normed_in)
        d_gain_one = lax.optimization_barrier(jnp.sum(first_terms, axis=0))
        grad_in = d_resid + d_in_norm
        grads = (d_gain_one, d_query, d_key, d_value, d_outgate, d_lowrank, d_forget, d_bias, d_group, d_output, d_gain_two, d_gate, d_up, d_down)
        return (tuple((left + right for left, right in zip(totals, grads))), (result, grad_in))
    zero_init = (jnp.zeros((D,), jnp.float32), jnp.zeros((D, H * DK), jnp.float32), jnp.zeros((D, H * DK), jnp.float32), jnp.zeros((D, H * DV), jnp.float32), jnp.zeros((D, H * DV), jnp.float32), jnp.zeros((D, R), jnp.float32), jnp.zeros((R, H * DK), jnp.float32), jnp.zeros((H * DK,), jnp.float32), jnp.zeros((DV,), jnp.float32), jnp.zeros((H * DV, D), jnp.float32), jnp.zeros((D,), jnp.float32), jnp.zeros((D, FF), jnp.float32), jnp.zeros((D, FF), jnp.float32), jnp.zeros((FF, D), jnp.float32))
    totals, (block_out, grad_input) = lax.scan(one_sequence, zero_init, (x_in, cotangent))
    return (block_out, grad_input, totals[0], totals[1], totals[2], totals[3], totals[4], totals[5], totals[6], totals[7], totals[8], totals[9], totals[10], totals[11], totals[12], totals[13])
```

```python
from types import SimpleNamespace

import jax
import jax.numpy as jnp
from jax import lax
from jax.experimental import pallas as pl
from jax.experimental.pallas import tpu as pltpu
from jax.sharding import PartitionSpec as P

DK = 128
DV = 256
SPAN = 64
SEQ, HEAD, DP = "seq", "head", "dp"


epsilon = 1e-06
normalizer = 16.0
highest = lax.Precision.HIGHEST


def exchange(items, cid):
    groups = []
    for kind, axis, _ in items:
        for name in axis if kind in ("wg", "rs") else (axis,):
            if name not in groups:
                groups.append(name)
    names = []
    for group in groups:
        for name in group if isinstance(group, tuple) else (group,):
            if name not in names:
                names.append(name)
    size = {name: lax.axis_size(name) for name in names}
    for group in groups:
        if isinstance(group, tuple):
            size[group] = size[group[0]] * size[group[1]]
    out_shape, scratch = [], []
    dma = pltpu.SemaphoreType.DMA
    for kind, axis, arr in items:
        if kind in ("wg", "rs"):
            n, m = size[axis[0]], size[axis[1]]
            scratch += [dma((2, 2, n)), dma((2, 2, n, m))]
            if kind == "wg":
                out_shape.append(jax.ShapeDtypeStruct((n,) + arr.shape, arr.dtype))
                scratch.append(dma)
            else:
                out_shape.append(jax.ShapeDtypeStruct((m,) + arr.shape[1:], jnp.float32))
                scratch.append(pltpu.VMEM((2,) + arr.shape, arr.dtype))
                scratch.append(pltpu.VMEM((2,) + arr.shape, arr.dtype))
            continue
        n = size[axis]
        scratch.append(dma((2, n)))
        if kind == "ar":
            out_shape.append(jax.ShapeDtypeStruct(arr.shape, arr.dtype))
            scratch += [dma((2, n)), pltpu.VMEM(arr.shape, arr.dtype)]
        else:
            inner = arr.shape if kind == "ag" else arr.shape[1:]
            out_shape.append(jax.ShapeDtypeStruct((n,) + inner, arr.dtype))
            scratch.append(dma)

    def kernel(*refs):
        count = len(items)
        ins, outs, rest = refs[:count], refs[count : 2 * count], list(refs[2 * count :])
        me = {name: lax.axis_index(name) for name in names}
        for group in groups:
            if isinstance(group, tuple):
                me[group] = me[group[0]] * size[group[1]] + me[group[1]]

        def device(group, place):
            if isinstance(group, tuple):
                return {
                    group[0]: place // size[group[1]],
                    group[1]: lax.rem(place, size[group[1]]),
                }
            return {group: place}

        barrier = pltpu.get_barrier_semaphore()
        for group in groups:
            for k in range(1, size[group]):
                pl.semaphore_signal(
                    barrier,
                    inc=1,
                    device_id=device(group, lax.rem(me[group] + k, size[group])),
                    device_id_type=pl.DeviceIdType.MESH,
                )
        pl.semaphore_wait(barrier, sum(size[group] - 1 for group in groups))

        def remote(source, target, send, recv, group, place):
            return pltpu.make_async_remote_copy(
                src_ref=source,
                dst_ref=target,
                send_sem=send,
                recv_sem=recv,
                device_id=device(group, place),
                device_id_type=pl.DeviceIdType.MESH,
            )

        waits, chains, sums = [], [], []

        def chain_gather(src, dst, sems, sems_two, local, axis, arr):
            name, other = axis
            n, here, m, place = size[name], me[name], size[other], me[other]
            part = arr.shape[0] // m
            rows = pl.ds(pl.multiple_of(place * part, part), part)
            own = pltpu.make_async_copy(src, dst.at[here], local)
            own.start()
            waits.append(own.wait)

            def hop(way, step, source, index):
                to = here + 1 if way == 0 else here - 1
                return remote(
                    source,
                    dst.at[index, rows],
                    sems.at[way, 0, step],
                    sems.at[way, 1, step],
                    name,
                    to,
                )

            def guarded(ok, call):
                waits.append(lambda: pl.when(ok)(call))

            open_ends = (here < n - 1, here > 0)
            for way in range(2):
                @pl.when(open_ends[way])
                def _():
                    hop(way, 0, src.at[rows], here).start()

                guarded(
                    open_ends[way],
                    lambda way=way: hop(way, 0, src.at[rows], here).wait_send(),
                )

            def advance(step):
                for way in range(2):
                    came = here - 1 - step if way == 0 else here + 1 + step
                    ok = came >= 0 if way == 0 else came < n
                    on = jnp.logical_and(ok, open_ends[way])

                    def partners(way=way, came=came):
                        for j in range(1, m):
                            to = lax.rem(place + j, m)
                            whose = lax.rem(place + m - j, m)
                            piece = dst.at[came, rows]
                            theirs = dst.at[came, pl.ds(pl.multiple_of(whose * part, part), part)]
                            send, recv = sems_two.at[way, 0, step, j], sems_two.at[way, 1, step, j]
                            yield (
                                remote(piece, piece, send, recv, other, to),
                                remote(theirs, theirs, send, recv, other, to),
                            )

                    @pl.when(ok)
                    def _():
                        hop(way, step, dst.at[came, rows], came).wait_recv()

                    if step + 1 < n - 1:
                        @pl.when(on)
                        def _():
                            hop(way, step + 1, dst.at[came, rows], came).start()

                        guarded(
                            on,
                            lambda way=way, came=came: hop(
                                way, step + 1, dst.at[came, rows], came
                            ).wait_send(),
                        )

                    @pl.when(ok)
                    def _():
                        for copy, _ in partners():
                            copy.start()

                    def finish(partners=partners):
                        for copy, arrival in partners():
                            copy.wait_send()
                            arrival.wait_recv()

                    guarded(ok, finish)

            chains.append((n - 1, advance, lambda: None))

        def chain_sum(src, dst, sems, sems_two, land, held, axis, arr):
            name, other = axis
            n, here, m, place = size[name], me[name], size[other], me[other]
            tall = 16 if arr.shape[1] % 16 == 0 else arr.shape[1]
            turns = arr.shape[1] // tall

            def by_rows(call):
                def one(turn, carry):
                    call(pl.ds(pl.multiple_of(turn * tall, tall), tall))
                    return carry

                lax.fori_loop(0, turns, one, 0)

            def hop(way, step, source, index):
                to = here + 1 if way == 0 else here - 1
                return remote(
                    source,
                    land.at[way, index],
                    sems.at[way, 0, step],
                    sems.at[way, 1, step],
                    name,
                    to,
                )

            def guarded(ok, call):
                waits.append(lambda: pl.when(ok)(call))

            firsts = (here == 0, here == n - 1)

            def advance(step):
                for way in range(2):
                    goal = n - 1 - step if way == 0 else step
                    passing = here < goal if way == 0 else here > goal
                    inner = jnp.logical_and(passing, jnp.logical_not(firsts[way]))
                    first = jnp.logical_and(passing, firsts[way])

                    @pl.when(first)
                    def _():
                        if step > 0:
                            before = goal + 1 if way == 0 else goal - 1
                            hop(way, step - 1, src.at[before], before).wait_send()
                        hop(way, step, src.at[goal], goal).start()

                    if step == n - 2:
                        guarded(
                            first,
                            lambda way=way, goal=goal: hop(
                                way, step, src.at[goal], goal
                            ).wait_send(),
                        )

                    @pl.when(inner)
                    def _():
                        hop(way, step, land.at[way, goal], goal).wait_recv()

                        def add(rows):
                            held[way, goal, rows] = (
                                land[way, goal, rows].astype(jnp.float32)
                                + src[goal, rows].astype(jnp.float32)
                            ).astype(held.dtype)

                        by_rows(add)
                        hop(way, step, held.at[way, goal], goal).start()

                    guarded(
                        inner,
                        lambda way=way, goal=goal: hop(
                            way, step, held.at[way, goal], goal
                        ).wait_send(),
                    )

            def partners():
                for j in range(1, m):
                    to = lax.rem(place + j, m)
                    whose = lax.rem(place + m - j, m)
                    send, recv = sems_two.at[0, 0, 0, j], sems_two.at[0, 1, 0, j]
                    yield (
                        remote(dst.at[place], dst.at[place], send, recv, other, to),
                        remote(dst.at[whose], dst.at[whose], send, recv, other, to),
                    )

            def close():
                def start(rows):
                    dst[place, rows] = src[here, rows].astype(jnp.float32)

                by_rows(start)
                for way in range(2):
                    step = n - 1 - here if way == 0 else here

                    @pl.when(jnp.logical_not(firsts[way]))
                    def _():
                        hop(way, step, land.at[way, here], here).wait_recv()

                        def add(rows):
                            dst[place, rows] = dst[place, rows] + land[way, here, rows].astype(
                                jnp.float32
                            )

                        by_rows(add)

                for copy, _ in partners():
                    copy.start()
                for copy, arrival in partners():
                    waits.append(copy.wait_send)
                    waits.append(arrival.wait_recv)

            chains.append((n, advance, close))

        for (kind, axis, arr), src, dst in zip(items, ins, outs):
            if kind in ("wg", "rs"):
                extra = [rest.pop(0) for _ in range(3 if kind == "wg" else 4)]
                (chain_gather if kind == "wg" else chain_sum)(src, dst, *extra, axis, arr)
                continue
            sems = rest.pop(0)
            n, here = size[axis], me[axis]
            if kind == "ar":
                sems_two, land = rest.pop(0), rest.pop(0)
                sent = []
                for k in range(1, n):
                    peer = lax.rem(here + k, n)
                    came = lax.rem(here + n - k, n)
                    pair = sems.at[0, k], sems.at[1, k]
                    copy = remote(src.at[peer], land.at[here], *pair, axis, peer)
                    copy.start()
                    sent.append((copy, remote(land.at[came], land.at[came], *pair, axis, peer)))
                sums.append((src, dst, land, sems_two, axis, n, here, sent))
                continue
            local = rest.pop(0)

            def piece(place):
                if kind == "ag":
                    return src
                if isinstance(axis, tuple):
                    return src.at[place // size[axis[1]]]
                return src.at[place]

            own = pltpu.make_async_copy(piece(here), dst.at[here], local)
            own.start()
            waits.append(own.wait)
            for k in range(1, n):
                peer = lax.rem(here + k, n)
                came = lax.rem(here + n - k, n)
                pair = sems.at[0, k], sems.at[1, k]
                copy = remote(piece(peer), dst.at[here], *pair, axis, peer)
                copy.start()
                waits.append(copy.wait_send)
                waits.append(remote(dst.at[came], dst.at[came], *pair, axis, peer).wait_recv)

        def finish_sums():
            for src, dst, land, sems_two, axis, n, here, sent in sums:
                total = src[here].astype(jnp.float32)
                for k, (copy, arrival) in enumerate(sent, 1):
                    arrival.wait_recv()
                    total = total + land[lax.rem(here + n - k, n)].astype(jnp.float32)
                dst[here] = total.astype(dst.dtype)
                for k in range(1, n):
                    peer = lax.rem(here + k, n)
                    came = lax.rem(here + n - k, n)
                    pair = sems_two.at[0, k], sems_two.at[1, k]
                    copy = remote(dst.at[here], dst.at[here], *pair, axis, peer)
                    copy.start()
                    waits.append(copy.wait_send)
                    waits.append(
                        remote(dst.at[came], dst.at[came], *pair, axis, peer).wait_recv
                    )
                for copy, _ in sent:
                    waits.append(copy.wait_send)

        steps = max([entry[0] for entry in chains], default=0)
        for step in range(steps):
            if step == 1:
                finish_sums()
            for last, advance, _ in chains:
                if step < last:
                    advance(step)
        if steps < 2:
            finish_sums()
        for _, _, close in chains:
            close()
        for wait in waits:
            wait()

    def room(shape, dtype):
        item = jnp.dtype(dtype).itemsize
        lead = 1
        for extent in shape[:-2]:
            lead *= extent
        tile = 32 // item
        return lead * (-(-shape[-2] // tile) * tile) * (-(-shape[-1] // 128) * 128) * item

    total = sum(room(item[2].shape, item[2].dtype) for item in items)
    total += sum(room(shape.shape, shape.dtype) for shape in out_shape)
    for kind, _, arr in items:
        total += room(arr.shape, arr.dtype) * {"ar": 3, "rs": 4}.get(kind, 0)
    limit = min(60 * 2**20, total + total // 8 + 2 * 2**20)
    vmem = pl.BlockSpec(memory_space=pltpu.VMEM)
    return pl.pallas_call(
        kernel,
        out_shape=out_shape,
        in_specs=[vmem] * len(items),
        out_specs=[vmem] * len(items),
        scratch_shapes=scratch,
        compiler_params=pltpu.CompilerParams(
            collective_id=cid, has_side_effects=True, vmem_limit_bytes=limit
        ),
    )(*[item[2] for item in items])


def dot_t(left, right):
    return lax.dot_general(
        left, right, (((1,), (1,)), ((), ())), preferred_element_type=jnp.float32
    )


def dot_rows(left, right):
    return lax.dot_general(
        left, right, (((0,), (0,)), ((), ())), preferred_element_type=jnp.float32
    )


def product(left, right):
    return jnp.dot(left, right, preferred_element_type=jnp.float32)


def rms_rows(inputs):
    return lax.rsqrt(jnp.mean(inputs * inputs, axis=-1, keepdims=True) + epsilon)


def norm_back(inputs, scale, gain, grad):
    scaled = gain * grad
    gain_terms = grad * inputs * scale
    input_grad = scale * scaled - inputs * scale**3 * jnp.mean(
        scaled * inputs, axis=-1, keepdims=True
    )
    return (gain_terms, input_grad)


def mixer_block(queries, keys_in, values_in, log_decay, start_state):
    block_len = min(SPAN, queries.shape[0])
    blocks = queries.shape[0] // block_len

    def cut(array):
        return array.reshape(blocks, block_len, array.shape[-1])

    lower = jnp.tril(jnp.ones((block_len, block_len), jnp.float32))

    def block_step(carried, pieces):
        query_blk, key_blk, value_blk, decay_blk = pieces
        running = jnp.cumsum(decay_blk, axis=0)
        from_state = jnp.dot(query_blk * jnp.exp(running), carried, precision=highest)
        spread = (
            jnp.exp(jnp.minimum(running[:, None, :] - running[None, :, :], 0.0)) * lower[:, :, None]
        )
        scores = jnp.einsum("id,jd,ijd->ij", query_blk, key_blk, spread, precision=highest)
        inside = jnp.dot(scores, value_blk, precision=highest)
        ending = running[-1]
        weighted = key_blk * jnp.exp(ending[None, :] - running)
        carried = jnp.exp(ending)[:, None] * carried + jnp.dot(
            weighted.T, value_blk, precision=highest
        )
        return (carried, from_state + inside)

    final_state, outputs = lax.scan(
        jax.checkpoint(block_step),
        start_state,
        (cut(queries), cut(keys_in), cut(values_in), cut(log_decay)),
    )
    return (outputs.reshape(queries.shape[0], values_in.shape[-1]), final_state)


def on_device(
    x_in,
    cotangent,
    attn_gain,
    w_query,
    w_key,
    w_value,
    w_outgate,
    w_lowrank,
    w_forget,
    forget_bias,
    group_gain,
    w_output,
    mlp_gain,
    w_gate,
    w_up,
    w_down,
):
    seqs_here, tok_here, width = x_in.shape
    total_rows = seqs_here * tok_here
    bf16, f32 = jnp.bfloat16, jnp.float32
    n_seq, n_head, n_dp = lax.axis_size("seq"), lax.axis_size("head"), lax.axis_size("dp")
    seq_pos, head_pos = lax.axis_index("seq"), lax.axis_index("head")
    shard_rows = w_query.shape[0]
    part_rows = shard_rows // n_dp
    key_cols, val_cols, hidden = w_query.shape[1], w_value.shape[1], w_gate.shape[1]
    rank = w_lowrank.shape[1]
    heads_here = key_cols // DK
    head_scale = DK ** (-0.5)
    side = -(-(rank + 2) // 128) * 128
    packed = jnp.concatenate(
        (
            w_query,
            w_key,
            w_value,
            w_outgate,
            w_lowrank,
            attn_gain[:, None],
            mlp_gain[:, None],
            jnp.zeros((shard_rows, side - rank - 2), bf16),
            w_output.T,
        ),
        axis=1,
    )
    packed_mlp = jnp.concatenate((w_gate, w_up, w_down.T), axis=1)
    (weights,) = exchange([("wg", ("seq", "dp"), packed)], 0)
    weights = weights.reshape(width, -1)
    attn_cols = 2 * key_cols + 2 * val_cols
    w_attn = weights[:, :attn_cols]
    w_low = weights[:, attn_cols : attn_cols + side]
    wl_full = w_low[:, :rank]
    gain_first = w_low[:, rank].astype(f32)
    gain_second = w_low[:, rank + 1].astype(f32)
    at = attn_cols + side
    wo_t = weights[:, at : at + val_cols]
    forget_cols = lax.dynamic_slice_in_dim(w_forget, head_pos * key_cols, key_cols, 1)
    bias_cols = lax.dynamic_slice_in_dim(forget_bias, head_pos * key_cols, key_cols, 0)

    def heads_of(array, size):
        return array.reshape(seqs_here, tok_here, heads_here, size).transpose(0, 2, 1, 3)

    def rows_of(array):
        return array.transpose(0, 2, 1, 3).reshape(total_rows, -1)

    def spread_head(array):
        return array.astype(bf16).reshape(n_head, array.shape[0] // n_head, array.shape[1])

    def by_part(array):
        array = array.reshape(total_rows, n_seq, n_dp, part_rows)
        return array.transpose(2, 0, 1, 3).reshape(n_dp, total_rows, n_seq * part_rows)

    def all_rows(array):
        return array.reshape(n_dp * total_rows, -1)

    def grad_of(left, right):
        return dot_rows(all_rows(left), all_rows(right)).astype(bf16)

    flat_in = x_in.reshape(total_rows, width)
    flat_cot = cotangent.reshape(total_rows, width)
    scale_one = rms_rows(flat_in)
    normed_in = (flat_in * scale_one * gain_first).astype(bf16)
    proj = product(normed_in, w_attn)
    q_rows = proj[:, :key_cols]
    k_rows = proj[:, key_cols : 2 * key_cols]
    v_rows = proj[:, 2 * key_cols : 2 * key_cols + val_cols]
    og_rows = proj[:, 2 * key_cols + val_cols :]
    low_rank = product(normed_in, wl_full)
    pre_gate = jnp.dot(low_rank, forget_cols, precision=highest) + bias_cols
    log_decay = jax.nn.log_sigmoid(pre_gate) / normalizer
    q_heads = heads_of(q_rows, DK)
    k_heads = heads_of(k_rows, DK)
    v_heads = heads_of(v_rows, DV)
    decay_heads = heads_of(log_decay, DK)
    running = jnp.cumsum(decay_heads, axis=2)
    ending = running[:, :, -1, :]
    decay_total = jnp.exp(ending)
    local_state = jnp.einsum(
        "shld,shlv->shdv",
        k_heads * jnp.exp(ending[:, :, None, :] - running),
        v_heads,
        precision=highest,
    )
    state_shape = local_state.shape
    states, decays = exchange(
        [
            ("ag", "seq", local_state.astype(bf16).reshape(-1, DV)),
            ("ag", "seq", jnp.broadcast_to(decay_total.reshape(1, -1), (8, decay_total.size))),
        ],
        1,
    )
    decays = decays[:, 0].reshape((n_seq,) + decay_total.shape)
    states = states.reshape((n_seq,) + state_shape)
    start_state = jnp.zeros(state_shape, f32)
    for j in range(n_seq - 1):
        start_state = jnp.where(
            j < seq_pos, decays[j][..., None] * start_state + states[j].astype(f32), start_state
        )

    def mixed(q_part, k_part, v_part, d_part):
        return jax.vmap(jax.vmap(mixer_block))(
            q_part * head_scale, k_part, v_part, d_part, start_state
        )

    (o_heads, end_state), pullback = jax.vjp(mixed, q_heads, k_heads, v_heads, decay_heads)
    gate_heads = heads_of(og_rows, DV)
    scale_three = rms_rows(o_heads)
    gated_norm = o_heads * scale_three * group_gain
    gate_sig = jax.nn.sigmoid(gate_heads)
    gate_act = gate_heads * gate_sig
    mixed_out = rows_of(gated_norm * gate_act).astype(bf16)
    mix_sum, weights_mlp = exchange(
        [
            ("ar", "head", spread_head(dot_t(mixed_out, wo_t))),
            ("wg", ("seq", "dp"), packed_mlp),
        ],
        2,
    )
    weights_mlp = weights_mlp.reshape(width, -1)
    w_gu = weights_mlp[:, : 2 * hidden]
    wdown_t = weights_mlp[:, 2 * hidden :]
    resid = flat_in + mix_sum.reshape(total_rows, width).astype(f32)
    scale_two = rms_rows(resid)
    normed_mid = (resid * scale_two * gain_second).astype(bf16)
    both = product(normed_mid, w_gu)
    gate_pre, up_pre = both[:, :hidden], both[:, hidden:]
    gate_sigma = jax.nn.sigmoid(gate_pre)
    gate_silu = gate_pre * gate_sigma
    mlp_hidden = (gate_silu * up_pre).astype(bf16)
    grad_out_b = flat_cot.astype(bf16)
    d_hidden = product(grad_out_b, wdown_t)
    d_gate_pre = (d_hidden * up_pre * gate_sigma * (1.0 + gate_pre * (1.0 - gate_sigma))).astype(
        bf16
    )
    d_up_pre = (d_hidden * gate_silu).astype(bf16)
    d_both = jnp.concatenate((d_gate_pre, d_up_pre), axis=1)
    sums, mid_two, out_two, both_two, hidden_two = exchange(
        [
            (
                "ar",
                "head",
                spread_head(
                    jnp.concatenate((dot_t(mlp_hidden, wdown_t), dot_t(d_both, w_gu)), axis=0)
                ),
            ),
            ("a2a", "dp", by_part(normed_mid)),
            ("a2a", "dp", by_part(grad_out_b)),
            ("ag", "dp", d_both),
            ("ag", "dp", mlp_hidden),
        ],
        3,
    )
    sums = sums.reshape(2, total_rows, width).astype(f32)
    result = resid + sums[0]
    d_normed_mid = sums[1]
    gain_terms, d_resid_norm = norm_back(resid, scale_two, gain_second, d_normed_mid)
    d_gain_two = jnp.sum(gain_terms, axis=0)
    d_resid = flat_cot + d_resid_norm
    d_resid_b = d_resid.astype(bf16)
    d_mixed = heads_of(product(d_resid_b, wo_t), DV)
    d_norm_out = d_mixed * gate_act
    d_gate_heads = d_mixed * gated_norm * gate_sig * (1.0 + gate_heads * (1.0 - gate_sig))
    d_group = jnp.sum(d_norm_out * o_heads * scale_three, axis=(0, 1, 2))
    group_terms, d_o_heads = norm_back(o_heads, scale_three, group_gain, d_norm_out)
    state_grad = jnp.einsum(
        "shld,shlv->shdv", q_heads * head_scale * jnp.exp(running), d_o_heads, precision=highest
    )
    grads_in, mixed_two, resid_two = exchange(
        [
            ("ag", "seq", state_grad.astype(bf16).reshape(-1, DV)),
            ("ag", "dp", mixed_out),
            ("a2a", "dp", by_part(d_resid_b)),
        ],
        4,
    )
    grads_late = jnp.concatenate(
        (
            grad_of(resid_two, mixed_two),
            grad_of(mid_two, both_two),
            grad_of(out_two, hidden_two),
        ),
        axis=1,
    ).reshape(n_seq, part_rows, -1)
    grads_in = grads_in.reshape((n_seq,) + state_shape)
    later_grad = jnp.zeros(state_shape, f32)
    for j in range(n_seq - 1, 0, -1):
        later_grad = jnp.where(
            j > seq_pos, decays[j][..., None] * later_grad + grads_in[j].astype(f32), later_grad
        )
    d_q, d_k, d_v, d_decay = pullback((d_o_heads, later_grad))
    d_pre = rows_of(d_decay) / normalizer * jax.nn.sigmoid(-pre_gate)
    d_bias = jnp.sum(d_pre, axis=0)
    d_forget = jnp.dot(low_rank.T, d_pre, precision=highest)
    d_low_part = jnp.dot(d_pre, forget_cols.T, precision=highest)
    d_proj = jnp.concatenate(
        (
            rows_of(d_q).astype(bf16),
            rows_of(d_k).astype(bf16),
            rows_of(d_v).astype(bf16),
            rows_of(d_gate_heads).astype(bf16),
        ),
        axis=1,
    )
    d_in_part = jnp.concatenate(
        (dot_t(d_proj, w_attn), d_low_part, jnp.zeros((total_rows, side - rank), f32)), axis=1
    )
    group_rows = d_group.reshape(1, DV)
    if DV < key_cols:
        group_rows = jnp.pad(group_rows, ((0, 0), (0, key_cols - DV)))
    if DV > key_cols:
        group_rows = group_rows.reshape(-1, key_cols)
    used = rank + 1 + group_rows.shape[0]
    small = jnp.concatenate(
        (
            d_forget,
            d_bias[None, :],
            group_rows,
            jnp.zeros((-used % 8, key_cols), f32),
        ),
        axis=0,
    )
    grads_late, in_sum, small_all, in_two, proj_two = exchange(
        [
            ("rs", ("seq", "dp"), grads_late),
            ("ar", "head", spread_head(d_in_part)),
            ("ag", ("seq", "dp"), small),
            ("a2a", "dp", by_part(normed_in)),
            ("ag", "dp", d_proj),
        ],
        5,
    )
    in_sum = in_sum.reshape(total_rows, width + side)
    d_low_b = in_sum[:, width : width + rank]
    d_normed_in = in_sum[:, :width].astype(f32) + dot_t(d_low_b, wl_full)
    first_terms, d_in_norm = norm_back(flat_in, scale_one, gain_first, d_normed_in)
    d_gain_one = jnp.sum(first_terms, axis=0)
    grad_in = d_resid + d_in_norm

    grads_attn = grad_of(in_two, proj_two).reshape(n_seq, part_rows, -1)
    tall = jnp.concatenate(
        (
            dot_rows(d_low_b, normed_in),
            d_gain_one[None, :],
            d_gain_two[None, :],
            jnp.zeros((-(rank + 2) % 8, width), f32),
        ),
        axis=0,
    )
    tall = tall.reshape(-1, n_seq, shard_rows).transpose(1, 0, 2)
    grads_attn, tall, small = exchange(
        [
            ("rs", ("seq", "dp"), grads_attn),
            ("a2a", ("seq", "dp"), tall),
            ("ag", "head", jnp.sum(small_all, axis=0)),
        ],
        6,
    )
    grads_attn = grads_attn.reshape(shard_rows, -1)
    grads_late = grads_late.reshape(shard_rows, -1)
    tall = jnp.sum(tall, axis=0)
    s_forget = small[:, :rank].transpose(1, 0, 2).reshape(rank, -1)
    s_bias = small[:, rank].reshape(-1)
    s_group = jnp.sum(small[:, rank + 1 : used], axis=0).reshape(-1)[:DV]
    s_query, s_key, s_value, s_outgate = jnp.split(
        grads_attn, [key_cols, 2 * key_cols, 2 * key_cols + val_cols], axis=1
    )
    s_output, s_gate, s_up, s_down = jnp.split(
        grads_late, [val_cols, val_cols + hidden, val_cols + 2 * hidden], axis=1
    )
    return (
        result.reshape(seqs_here, tok_here, width),
        grad_in.reshape(seqs_here, tok_here, width),
        tall[rank],
        s_query,
        s_key,
        s_value,
        s_outgate,
        tall[:rank].T,
        s_forget,
        s_bias,
        s_group,
        s_output.T,
        tall[rank + 1],
        s_gate,
        s_up,
        s_down.T,
    )


def fused_layer(axes, dims, args):
    n, nh, nd = axes
    tok, width, shard, kc, vc, hid, rank = dims
    bf16, f32 = jnp.bfloat16, jnp.float32
    half = shard // 2
    nhalf = n * half
    acols = 2 * kc + 2 * vc
    cuts = ((0, kc), (kc, kc), (2 * kc, vc), (2 * kc + vc, vc))
    qrows = tok // nh
    hhid = hid // 2
    hkv = vc // 2
    scale = DK ** (-0.5)
    levels = []
    size = tok // 2
    while size:
        levels.append(size)
        size //= 2
    nl = len(levels) + 2
    srows = rank * 2
    trows = -(-(rank + 2) // 8) * 8
    grow = vc // kc
    mrows = -(-(rank + 1 + grow) // 8) * 8
    dma = pltpu.SemaphoreType.DMA
    n_gather = 6
    n_sum = 5
    n_ar = 4

    out_shape = [
        jax.ShapeDtypeStruct((tok, width), f32),
        jax.ShapeDtypeStruct((tok, width), f32),
        jax.ShapeDtypeStruct((shard, kc), f32),
        jax.ShapeDtypeStruct((shard, kc), f32),
        jax.ShapeDtypeStruct((shard, vc), f32),
        jax.ShapeDtypeStruct((shard, vc), f32),
        jax.ShapeDtypeStruct((vc, shard), f32),
        jax.ShapeDtypeStruct((hid, shard), f32),
        jax.ShapeDtypeStruct((hid, shard), f32),
        jax.ShapeDtypeStruct((hid, shard), f32),
        jax.ShapeDtypeStruct((rank, shard), f32),
        jax.ShapeDtypeStruct((1, shard), f32),
        jax.ShapeDtypeStruct((1, shard), f32),
        jax.ShapeDtypeStruct((rank, nh * kc), f32),
        jax.ShapeDtypeStruct((1, nh * kc), f32),
        jax.ShapeDtypeStruct((1, vc), f32),
    ]
    anys = pl.BlockSpec(memory_space=pl.ANY)
    vmem = pl.BlockSpec(memory_space=pltpu.VMEM)
    out_specs = [anys] * 10 + [vmem] * 6
    in_specs = [anys] * 7 + [vmem] * 3 + [anys] * 4

    shapes = dict(
        X=((tok, width), f32),
        COT=((tok, width), f32),
        WA=((width, acols), bf16),
        SIDE=((srows, width), bf16),
        WO=((vc, width), bf16),
        WG=((hid, width), bf16),
        WU=((hid, width), bf16),
        WD=((hid, width), bf16),
        XS=((nl, tok, DK), f32),
        GS=((nl * tok, DK), f32),
        QKVO=((tok, acols), f32),
        PRE=((tok, kc), f32),
        LOW=((tok, rank), f32),
        AM=((tok, tok), f32),
        ST=((vc, DK), bf16),
        STL=((n, vc, DK), bf16),
        DEC=((8, DK), f32),
        DECL=((n, 8, DK), f32),
        S0=((vc, DK), f32),
        SG=((vc, DK), bf16),
        SGL=((n, vc, DK), bf16),
        LG=((vc, DK), f32),
        O=((tok, vc), f32),
        HRES=((tok, width), f32),
        HN=((tok, width), bf16),
        DRES=((tok, width), f32),
        XN=((tok, width), bf16),
        DMIX=((tok, vc), f32),
        AST0=((nh, qrows, width), bf16),
        ALD0=((nh, qrows, width), bf16),
        ASM0=((nh, qrows, width), bf16),
        AST1=((nh, qrows, width), bf16),
        ALD1=((nh, qrows, width), bf16),
        ASM1=((nh, qrows, width), bf16),
        AST2=((nh, qrows, width), bf16),
        ALD2=((nh, qrows, width), bf16),
        ASM2=((nh, qrows, width), bf16),
        AST3=((nh, qrows, width + 128), bf16),
        ALD3=((nh, qrows, width + 128), bf16),
        ASM3=((nh, qrows, width + 128), bf16),
        HN2=((2 * tok, nhalf), bf16),
        HNO=((tok, nhalf), bf16),
        GO2=((2 * tok, nhalf), bf16),
        GOO=((tok, nhalf), bf16),
        DY2=((2 * tok, nhalf), bf16),
        DYO=((tok, nhalf), bf16),
        XN2=((2 * tok, nhalf), bf16),
        XNO=((tok, nhalf), bf16),
        DA1=((2 * tok, hid), bf16),
        DA2=((2 * tok, hid), bf16),
        MM=((2 * tok, hid), bf16),
        ZZ=((2 * tok, vc), bf16),
        DP=((2 * tok, acols), bf16),
        RG=((hid, nhalf), bf16),
        RU=((hid, nhalf), bf16),
        RD=((hid, nhalf), bf16),
        RO=((vc, nhalf), bf16),
        RA=((nhalf, acols), bf16),
        LG_=((2, 3, hid, half), bf16),
        LU_=((2, 3, hid, half), bf16),
        LD_=((2, 3, hid, half), bf16),
        LO_=((2, 3, vc, half), bf16),
        LA_=((2, 3, half, acols), bf16),
        FG=((hid, half), f32),
        FU=((hid, half), f32),
        FD=((hid, half), f32),
        FO=((vc, half), f32),
        FA=((half, acols), f32),
        BOUT=((tok, width), f32),
        GIN=((tok, width), f32),
        TALL=((n, trows, shard), f32),
        TALLL=((n * nd, trows, shard), f32),
        SMALL=((mrows, kc), f32),
        SMALLL=((n * nd, mrows, kc), f32),
        SMH=((mrows, kc), f32),
        SMHL=((nh, mrows, kc), f32),
    )
    names = list(shapes)
    scratch = [pltpu.VMEM(*shapes[name]) for name in names]
    sem_shapes = dict(
        load=(12,),
        gat=(n_gather, 2, 2, n - 1),
        gtwo=(n_gather, 2, 2, n - 1),
        st=(2, n),
        dec=(2, n),
        sg=(2, n),
        ara=(n_ar, 2, nh),
        arb=(n_ar, 2, nh),
        act=(2, 9),
        rs=(n_sum, 2, 2, 3),
        outl=(12,),
        outr=(2, 8),
        tall=(2, n * nd),
        small=(2, n * nd),
        smh=(2, nh),
    )
    sem_names = list(sem_shapes)
    scratch += [dma(sem_shapes[name]) for name in sem_names]

    def kernel(*refs):
        (x_h, cot_h, side_h, wq_h, wk_h, wv_h, wog_h, wf_r, fb_r, gg_r, wo_h, wg_h, wu_h, wd_h) = refs[:14]
        outs = refs[14:30]
        (bout_h, gin_h, gq_h, gk_h, gv_h, gog_h, gwo_h, gg_h, gu_h, gd_h) = outs[:10]
        (low_o, again_o, mgain_o, forget_o, bias_o, group_o) = outs[10:]
        R = SimpleNamespace(**dict(zip(names, refs[30 : 30 + len(names)])))
        S = SimpleNamespace(**dict(zip(sem_names, refs[30 + len(names) :])))
        me, hh, dd = lax.axis_index(SEQ), lax.axis_index(HEAD), lax.axis_index(DP)
        other = 1 - dd
        mesh_id = pl.DeviceIdType.MESH

        def remote(src, dst, send, recv, to):
            return pltpu.make_async_remote_copy(
                src_ref=src, dst_ref=dst, send_sem=send, recv_sem=recv, device_id=to, device_id_type=mesh_id
            )

        def mult(value, by):
            return pl.multiple_of(value * by, by)

        def lanes_of(place):
            return pl.ds(mult(place, shard), shard)

        late = []

        rows_me = pl.ds(mult(me, shard), shard)
        loads = [
            (wq_h, R.WA.at[rows_me, 0:kc]),
            (wk_h, R.WA.at[rows_me, kc : 2 * kc]),
            (wv_h, R.WA.at[rows_me, 2 * kc : 2 * kc + vc]),
            (wog_h, R.WA.at[rows_me, 2 * kc + vc : acols]),
            (side_h, R.SIDE.at[:, lanes_of(me)]),
            (x_h, R.X),
            (wo_h, R.WO.at[:, lanes_of(me)]),
            (wg_h, R.WG.at[:, lanes_of(me)]),
            (wu_h, R.WU.at[:, lanes_of(me)]),
            (wd_h, R.WD.at[:, lanes_of(me)]),
            (cot_h, R.COT),
        ]
        loads = [pltpu.make_async_copy(a, b, S.load.at[i]) for i, (a, b) in enumerate(loads)]
        for copy in loads:
            copy.start()

        barrier = pltpu.get_barrier_semaphore()
        count = 0
        for k in range(1, nh):
            pl.semaphore_signal(barrier, inc=1, device_id={HEAD: lax.rem(hh + k, nh)}, device_id_type=mesh_id)
            count += 1
        flat = me * nd + dd
        for k in range(1, n * nd):
            peer = lax.rem(flat + k, n * nd)
            pl.semaphore_signal(
                barrier, inc=1, device_id={SEQ: peer // nd, DP: lax.rem(peer, nd)}, device_id_type=mesh_id
            )
            count += 1
        pl.semaphore_wait(barrier, count)

        def rows_view(ref, c, d):
            return ref.at[pl.ds(pl.multiple_of(c * shard + d * half, half), half)]

        def lane_view(rows):
            return lambda ref, c, d: ref.at[pl.ds(mult(d, rows), rows), lanes_of(c)]

        pieces = [
            (R.WA, rows_view),
            (R.SIDE, lane_view(rank)),
            (R.WO, lane_view(hkv)),
            (R.WG, lane_view(hhid)),
            (R.WU, lane_view(hhid)),
            (R.WD, lane_view(hhid)),
        ]
        open_ends = (me < n - 1, me > 0)

        def guarded(ok, call):
            late.append(lambda: pl.when(ok)(call))

        def g_hop(p, way, step, c):
            ref, view = pieces[p]
            v = view(ref, c, dd)
            return remote(v, v, S.gat.at[p, way, 0, step], S.gat.at[p, way, 1, step], {SEQ: me + 1 if way == 0 else me - 1})

        def g_pair(p, way, step, c, d):
            ref, view = pieces[p]
            v = view(ref, c, d)
            return remote(v, v, S.gtwo.at[p, way, 0, step], S.gtwo.at[p, way, 1, step], {DP: other})

        def d_send(p, way, dist):
            ref, view = pieces[p]
            v = view(ref, me, dd)
            to = me + dist if way == 0 else me - dist
            return remote(v, v, S.gat.at[p, way, 0, dist - 1], S.gat.at[p, way, 1, dist - 1], {SEQ: to})

        def reach(way, dist):
            return me + dist < n if way == 0 else me - dist >= 0

        def d_own(p):
            for dist in range(min(2, n - 1), 0, -1):
                for way in range(2):
                    ok = reach(way, dist)
                    pl.when(ok)(lambda way=way, dist=dist: d_send(p, way, dist).start())
                    guarded(ok, lambda way=way, dist=dist: d_send(p, way, dist).wait_send())

        def d_take(p, dist):
            if dist >= n:
                return
            for way in range(2):
                c, ok = came_of(way, dist - 1)
                pl.when(ok)(lambda way=way, c=c: g_hop(p, way, dist - 1, c).wait_recv())
                if dist == 2 and n > 3:
                    on = jnp.logical_and(ok, open_ends[way])
                    pl.when(on)(lambda way=way, c=c: g_hop(p, way, 2, c).start())
                    guarded(on, lambda way=way, c=c: g_hop(p, way, 2, c).wait_send())
                pl.when(ok)(lambda way=way, c=c: g_pair(p, way, dist - 1, c, dd).start())
                guarded(ok, lambda way=way, c=c: g_pair(p, way, dist - 1, c, dd).wait_send())

        def came_of(way, step):
            c = me - 1 - step if way == 0 else me + 1 + step
            return c, (c >= 0 if way == 0 else c < n)

        def g_own(p):
            for way in range(2):
                pl.when(open_ends[way])(lambda way=way: g_hop(p, way, 0, me).start())
                guarded(open_ends[way], lambda way=way: g_hop(p, way, 0, me).wait_send())

        def g_step(p, step):
            for way in range(2):
                c, ok = came_of(way, step)
                on = jnp.logical_and(ok, open_ends[way])
                pl.when(ok)(lambda way=way, c=c: g_hop(p, way, step, c).wait_recv())
                if step + 1 < n - 1:
                    pl.when(on)(lambda way=way, c=c: g_hop(p, way, step + 1, c).start())
                    guarded(on, lambda way=way, c=c: g_hop(p, way, step + 1, c).wait_send())
                pl.when(ok)(lambda way=way, c=c: g_pair(p, way, step, c, dd).start())
                guarded(ok, lambda way=way, c=c: g_pair(p, way, step, c, dd).wait_send())

        def g_end(p):
            for step in range(n - 1):
                for way in range(2):
                    c, ok = came_of(way, step)
                    pl.when(ok)(lambda way=way, c=c, step=step: g_pair(p, way, step, c, other).wait_recv())

        heads = (
            (R.AST0, R.ALD0, R.ASM0),
            (R.AST1, R.ALD1, R.ASM1),
            (R.AST2, R.ALD2, R.ASM2),
            (R.AST3, R.ALD3, R.ASM3),
        )

        def ar_refs(k):
            return heads[k]

        def ar_pair(k, sems, src, dst, j, to):
            return remote(src, dst, sems.at[k, 0, j], sems.at[k, 1, j], {HEAD: to})

        def ar_start(k):
            src, land, _ = ar_refs(k)
            for j in range(1, nh):
                to = lax.rem(hh + j, nh)
                copy = ar_pair(k, S.ara, src.at[to], land.at[hh], j, to)
                copy.start()
                late.append(copy.wait_send)

        def ar_mid(k):
            src, land, dst = ar_refs(k)
            total = src[hh].astype(f32)
            for j in range(1, nh):
                came = lax.rem(hh + nh - j, nh)
                ar_pair(k, S.ara, land.at[came], land.at[came], j, came).wait_recv()
                total = total + land[came].astype(f32)
            dst[hh] = total.astype(bf16)
            for j in range(1, nh):
                to = lax.rem(hh + j, nh)
                copy = ar_pair(k, S.arb, dst.at[hh], dst.at[hh], j, to)
                copy.start()
                late.append(copy.wait_send)

        def ar_end(k):
            dst = ar_refs(k)[2]
            for j in range(1, nh):
                came = lax.rem(hh + nh - j, nh)
                ar_pair(k, S.arb, dst.at[came], dst.at[came], j, came).wait_recv()

        def ar_fill(k, value):
            src = ar_refs(k)[0]
            for j in range(nh):
                src[j, :, : value.shape[1]] = value[j * qrows : (j + 1) * qrows].astype(bf16)

        def ar_value(k, cols=width):
            dst = ar_refs(k)[2]
            return jnp.concatenate([dst[j, :, :cols] for j in range(nh)], axis=0).astype(f32)

        def act_send(i, src, dst):
            copy = remote(src, dst, S.act.at[0, i], S.act.at[1, i], {DP: other})
            copy.start()
            late.append(copy.wait_send)

        def act_wait(i, src, dst):
            remote(src, dst, S.act.at[0, i], S.act.at[1, i], {DP: other}).wait_recv()

        top, low_rows = pl.ds(0, tok), pl.ds(tok, tok)

        def split(value, mine, theirs):
            for z in range(n):
                lo = value[:, z * shard : z * shard + half]
                hi = value[:, z * shard + half : (z + 1) * shard]
                first = dd == 0
                mine[0:tok, z * half : (z + 1) * half] = jnp.where(first, lo, hi)
                theirs[:, z * half : (z + 1) * half] = jnp.where(first, hi, lo)

        sums = [
            (R.RG, R.LG_, R.FG, True),
            (R.RU, R.LU_, R.FU, True),
            (R.RD, R.LD_, R.FD, True),
            (R.RO, R.LO_, R.FO, True),
            (R.RA, R.LA_, R.FA, False),
        ]

        def chunk(p, g):
            ref, kind = sums[p][0], sums[p][3]
            at = g * half if isinstance(g, int) else mult(g, half)
            if kind:
                return ref.at[:, pl.ds(at, half)]
            return ref.at[pl.ds(at, half)]

        def r_send(p, way, slot, src, to):
            return remote(
                src, sums[p][1].at[way, slot], S.rs.at[p, way, 0, slot], S.rs.at[p, way, 1, slot], {SEQ: to}
            )

        ends = (me == 0, me == n - 1)
        seconds = (me == 1, me == n - 2)

        def r_start(p, way):
            far = n - 1 if way == 0 else 0
            step = 1 if way == 0 else -1
            if n > 3:
                pl.when(ends[way])(lambda: r_send(p, way, 2, chunk(p, far), me + step).start())
                guarded(ends[way], lambda: r_send(p, way, 2, chunk(p, far), me + step).wait_send())
            for dist in range(min(2, n - 1), 0, -1):
                ok = reach(way, dist)
                if dist == 2 and n > 3:
                    ok = jnp.logical_and(ok, jnp.logical_not(seconds[way]))
                to = me + dist * step
                pl.when(ok)(lambda dist=dist, to=to: r_send(p, way, dist - 1, chunk(p, to), to).start())
                guarded(ok, lambda dist=dist, to=to: r_send(p, way, dist - 1, chunk(p, to), to).wait_send())

        def r_relay(p):
            land = sums[p][1]
            if n > 3:
                for way in range(2):
                    far = n - 1 if way == 0 else 0

                    @pl.when(seconds[way])
                    def _():
                        r_send(p, way, 2, land.at[way, 2], me).wait_recv()
                        land[way, 2] = (land[way, 2].astype(f32) + chunk(p, far)[...].astype(f32)).astype(bf16)
                        r_send(p, way, 1, land.at[way, 2], far).start()

                    guarded(seconds[way], lambda way=way, far=far: r_send(p, way, 1, land.at[way, 2], far).wait_send())

        def r_close(p):
            land, fin = sums[p][1], sums[p][2]
            fin[...] = chunk(p, me)[...].astype(f32)
            for dist in range(1, min(2, n - 1) + 1):
                for way in range(2):

                    @pl.when(reach(1 - way, dist))
                    def _():
                        r_send(p, way, dist - 1, land.at[way, dist - 1], me).wait_recv()
                        fin[...] = fin[...] + land[way, dist - 1].astype(f32)

        outputs = [
            (R.FG, gg_h, True),
            (R.FU, gu_h, True),
            (R.FD, gd_h, True),
            (R.FO, gwo_h, True),
        ] + [(R.FA.at[:, at : at + w], ref, False) for (at, w), ref in zip(cuts, (gq_h, gk_h, gv_h, gog_h))]

        def out_view(ref, kind, d):
            place = pl.ds(mult(d, half), half)
            return ref.at[:, place] if kind else ref.at[place]

        def put(i):
            src, ref, kind = outputs[i]
            view = out_view(ref, kind, dd)
            copy = pltpu.make_async_copy(src, view, S.outl.at[i])
            copy.start()
            late.append(copy.wait)
            copy = remote(src, view, S.outr.at[0, i], S.outr.at[1, i], {DP: other})
            copy.start()
            late.append(copy.wait_send)
            theirs = out_view(ref, kind, other)
            late.append(remote(theirs, theirs, S.outr.at[0, i], S.outr.at[1, i], {DP: other}).wait_recv)

        def put_local(i, src, ref):
            copy = pltpu.make_async_copy(src, ref, S.outl.at[i])
            copy.start()
            late.append(copy.wait)

        def hdot(a, b):
            return jnp.dot(a, b, precision=highest, preferred_element_type=f32)

        def hdot_t(a, b):
            return lax.dot_general(a, b, (((1,), (1,)), ((), ())), precision=highest, preferred_element_type=f32)

        def hdot_rows(a, b):
            return lax.dot_general(a, b, (((0,), (0,)), ((), ())), precision=highest, preferred_element_type=f32)

        def iota(axis):
            return lax.broadcasted_iota(jnp.int32, (tok, tok), axis)

        def span(level, i, t):
            if level == nl - 2:
                return t <= i
            if level == nl - 1:
                return t > i
            b = levels[level]
            r = (i & ~(2 * b - 1)) + (b - 1)
            upper = (i & b) != 0
            return jnp.logical_or(
                jnp.logical_and(upper, jnp.logical_and(t > r, t <= i)),
                jnp.logical_and(jnp.logical_not(upper), jnp.logical_and(t > i, t <= r)),
            )

        def mask_of(level):
            b = levels[level]
            i, j = iota(0), iota(1)
            same = (i & ~(2 * b - 1)) == (j & ~(2 * b - 1))
            return jnp.logical_and(same, jnp.logical_and((i & b) != 0, (j & b) == 0))

        def upper_rows(level):
            return (lax.broadcasted_iota(jnp.int32, (tok, DK), 0) & levels[level]) != 0

        for copy in loads[:5]:
            copy.wait()
        g_own(1)
        g_own(0)
        loads[5].wait()
        x = R.X[...]
        scale_one = lax.rsqrt(jnp.mean(x * x, axis=-1, keepdims=True) + epsilon)
        for step in range(n - 1):
            g_step(1, step)
            g_step(0, step)
        for copy in loads[6:]:
            copy.wait()
        d_own(2)
        d_own(3)
        g_end(1)
        gain_first = R.SIDE[rank : rank + 1].astype(f32)
        normed = (x * scale_one * gain_first).astype(bf16)
        R.XN[...] = normed
        low = dot_t(normed, R.SIDE[0:rank])
        R.LOW[...] = low
        fcols = pl.ds(mult(hh, kc), kc)
        pre = hdot(low, wf_r[:, fcols]) + fb_r[:, fcols]
        R.PRE[...] = pre
        decay = (jnp.minimum(pre, 0.0) - jnp.log1p(jnp.exp(-jnp.abs(pre)))) / normalizer
        for level in range(nl):
            ones = jnp.where(span(level, iota(0), iota(1)), 1.0, 0.0).astype(f32)
            R.XS[level] = jnp.exp(hdot(ones, decay))
        total_decay = jnp.exp(jnp.sum(decay, axis=0, keepdims=True))
        R.DEC[...] = jnp.broadcast_to(total_decay, (8, DK))
        g_end(0)
        R.QKVO[...] = product(normed, R.WA[...])
        keys = R.QKVO[:, kc : 2 * kc]
        values = R.QKVO[:, 2 * kc : 2 * kc + vc]
        R.ST[...] = hdot_rows(values, keys * R.XS[nl - 1]).astype(bf16)

        def seq_pair(sems, src, dst, k, to):
            return remote(src, dst, sems.at[0, k], sems.at[1, k], {SEQ: to})

        for k in range(1, n):
            to = lax.rem(me + k, n)
            copy = seq_pair(S.dec, R.DEC, R.DECL.at[me], k, to)
            copy.start()
            late.append(copy.wait_send)
            ok = me + k < n
            pl.when(ok)(lambda k=k: seq_pair(S.st, R.ST, R.STL.at[me], k, me + k).start())
            guarded(ok, lambda k=k: seq_pair(S.st, R.ST, R.STL.at[me], k, me + k).wait_send())
        d_own(4)
        d_own(5)

        queries = R.QKVO[:, 0:kc] * scale
        i, j = iota(0), iota(1)
        scores = jnp.where(i == j, jnp.sum(queries * keys, axis=-1, keepdims=True), 0.0)
        for level in range(nl - 2):
            xs = R.XS[level]
            up = upper_rows(level)
            part = hdot_t(jnp.where(up, queries * xs, 0.0), jnp.where(up, 0.0, keys * xs))
            scores = jnp.where(mask_of(level), part, scores)
        R.AM[...] = scores
        inside = hdot(scores, values)
        split(R.XN[...], R.XN2, R.XNO)
        split(R.COT[...].astype(bf16), R.GO2, R.GOO)
        act_send(0, R.XNO, R.XN2.at[low_rows])
        act_send(1, R.GOO, R.GO2.at[low_rows])
        d_take(2, 1)
        d_take(2, 2)
        d_take(3, 2)

        for k in range(1, n):
            came = lax.rem(me + n - k, n)
            seq_pair(S.dec, R.DECL.at[came], R.DECL.at[came], k, came).wait_recv()
        R.S0[...] = jnp.zeros((vc, DK), f32)
        for k in range(n - 1, 0, -1):

            @pl.when(me - k >= 0)
            def _():
                src = me - k
                seq_pair(S.st, R.STL.at[src], R.STL.at[src], k, src).wait_recv()
                R.S0[...] = R.DECL[src, 0:1, :] * R.S0[...] + R.STL[src].astype(f32)

        out = hdot_t(queries * R.XS[nl - 2], R.S0[...]) + inside
        R.O[...] = out
        gate = R.QKVO[:, 2 * kc + vc : acols]
        sig3 = lax.logistic(gate)
        scale_three = lax.rsqrt(jnp.mean(out * out, axis=-1, keepdims=True) + epsilon)
        mixed = (out * scale_three * gg_r[...] * (gate * sig3)).astype(bf16)
        R.ZZ[0:tok] = mixed
        d_take(2, 3)
        g_end(2)
        ar_fill(0, product(mixed, R.WO[...]))
        ar_start(0)
        act_send(2, R.ZZ.at[top], R.ZZ.at[low_rows])
        d_take(3, 1)
        ar_mid(0)
        d_take(4, 2)
        ar_end(0)
        hres = R.X[...] + ar_value(0)
        R.HRES[...] = hres
        scale_two = lax.rsqrt(jnp.mean(hres * hres, axis=-1, keepdims=True) + epsilon)
        gain_second = R.SIDE[rank + 1 : rank + 2].astype(f32)
        hn = (hres * scale_two * gain_second).astype(bf16)
        R.HN[...] = hn
        split(hn, R.HN2, R.HNO)
        act_send(3, R.HNO, R.HN2.at[low_rows])
        d_take(5, 2)
        d_take(4, 1)
        d_take(3, 3)
        d_take(5, 1)
        d_take(4, 3)
        g_end(3)
        g_end(4)
        a1 = dot_t(R.HN[...], R.WG[...])
        a2 = dot_t(R.HN[...], R.WU[...])
        d_take(5, 3)
        g_end(5)
        d_hid = dot_t(R.COT[...].astype(bf16), R.WD[...])
        s1 = lax.logistic(a1)
        silu = a1 * s1
        R.MM[0:tok] = (silu * a2).astype(bf16)
        R.DA1[0:tok] = (d_hid * a2 * s1 * (1.0 + a1 * (1.0 - s1))).astype(bf16)
        R.DA2[0:tok] = (d_hid * silu).astype(bf16)
        ar_fill(1, product(R.DA1[0:tok], R.WG[...]) + product(R.DA2[0:tok], R.WU[...]))
        ar_start(1)
        act_send(4, R.DA1.at[top], R.DA1.at[low_rows])
        act_send(5, R.DA2.at[top], R.DA2.at[low_rows])
        act_send(6, R.MM.at[top], R.MM.at[low_rows])
        ar_fill(2, product(R.MM[0:tok], R.WD[...]))
        act_wait(1, R.GOO, R.GO2.at[low_rows])
        act_wait(3, R.HNO, R.HN2.at[low_rows])
        act_wait(4, R.DA1.at[top], R.DA1.at[low_rows])
        R.RG[...] = dot_rows(R.DA1[...], R.HN2[...]).astype(bf16)
        r_start(0, 0)
        r_start(0, 1)
        ar_mid(1)
        ar_start(2)
        act_wait(5, R.DA2.at[top], R.DA2.at[low_rows])
        R.RU[...] = dot_rows(R.DA2[...], R.HN2[...]).astype(bf16)
        r_start(1, 0)
        act_wait(6, R.MM.at[top], R.MM.at[low_rows])
        R.RD[...] = dot_rows(R.MM[...], R.GO2[...]).astype(bf16)
        r_start(2, 0)
        ar_end(1)

        d_hn = ar_value(1)
        hres = R.HRES[...]
        scale_two = lax.rsqrt(jnp.mean(hres * hres, axis=-1, keepdims=True) + epsilon)
        terms, d_norm = norm_back(hres, scale_two, gain_second, d_hn)
        gain_two_grad = jnp.sum(terms, axis=0, keepdims=True)
        d_res = R.COT[...] + d_norm
        R.DRES[...] = d_res
        dy = d_res.astype(bf16)
        d_mixed = dot_t(dy, R.WO[...])
        ar_mid(2)
        out = R.O[...]
        gate = R.QKVO[:, 2 * kc + vc : acols]
        sig3 = lax.logistic(gate)
        scale_three = lax.rsqrt(jnp.mean(out * out, axis=-1, keepdims=True) + epsilon)
        normed_out = out * scale_three * gg_r[...]
        d_on = d_mixed * (gate * sig3)
        d_gate = d_mixed * normed_out * sig3 * (1.0 + gate * (1.0 - sig3))
        R.DP[0:tok, 2 * kc + vc : acols] = d_gate.astype(bf16)
        group_terms, d_out = norm_back(out, scale_three, gg_r[...], d_on)
        group_row = jnp.sum(group_terms, axis=0, keepdims=True)
        queries = R.QKVO[:, 0:kc] * scale
        keys = R.QKVO[:, kc : 2 * kc]
        values = R.QKVO[:, 2 * kc : 2 * kc + vc]
        R.DMIX[...] = d_out
        R.SG[...] = hdot_rows(d_out, queries * R.XS[nl - 2]).astype(bf16)
        for k in range(1, n):
            ok = me - k >= 0
            pl.when(ok)(lambda k=k: seq_pair(S.sg, R.SG, R.SGL.at[me], k, me - k).start())
            guarded(ok, lambda k=k: seq_pair(S.sg, R.SG, R.SGL.at[me], k, me - k).wait_send())
        r_start(1, 1)
        r_start(2, 1)
        split(dy, R.DY2, R.DYO)
        act_send(7, R.DYO, R.DY2.at[low_rows])

        d_out = R.DMIX[...]
        d_scores = hdot_t(d_out, values)
        i, j = iota(0), iota(1)
        diag = jnp.sum(jnp.where(i == j, d_scores, 0.0), axis=-1, keepdims=True)
        d_q = diag * keys
        d_k = diag * queries
        for level in range(nl - 2):
            xs = R.XS[level]
            up = upper_rows(level)
            part = jnp.where(mask_of(level), d_scores, 0.0)
            q_part = xs * hdot(part, jnp.where(up, 0.0, keys * xs))
            k_part = xs * hdot_rows(part, jnp.where(up, queries * xs, 0.0))
            R.GS[level * tok : (level + 1) * tok] = queries * q_part + keys * k_part
            d_q = d_q + q_part
            d_k = d_k + k_part
        q_part = R.XS[nl - 2] * hdot(d_out, R.S0[...])
        R.GS[(nl - 2) * tok : (nl - 1) * tok] = queries * q_part
        d_q = (d_q + q_part) * scale
        R.DP[0:tok, 0:kc] = d_q.astype(bf16)
        d_v = hdot_rows(R.AM[...], d_out)
        r_relay(0)
        R.LG[...] = jnp.zeros((vc, DK), f32)
        for k in range(n - 1, 0, -1):

            @pl.when(me + k < n)
            def _():
                src = me + k
                seq_pair(S.sg, R.SGL.at[src], R.SGL.at[src], k, src).wait_recv()
                R.LG[...] = R.DECL[src, 0:1, :] * R.LG[...] + R.SGL[src].astype(f32)

        later = R.LG[...]
        k_part = R.XS[nl - 1] * hdot(values, later)
        R.GS[(nl - 1) * tok : nl * tok] = keys * k_part
        R.DP[0:tok, kc : 2 * kc] = (d_k + k_part).astype(bf16)
        d_v = d_v + hdot_t(keys * R.XS[nl - 1], later)
        R.DP[0:tok, 2 * kc : 2 * kc + vc] = d_v.astype(bf16)
        act_send(8, R.DP.at[top], R.DP.at[low_rows])
        whole_row = R.DEC[0:1] * jnp.sum(R.S0[...] * later, axis=0, keepdims=True)
        d_decay = jnp.broadcast_to(whole_row, (tok, DK))
        for level in range(nl):
            ones = jnp.where(span(level, iota(1), iota(0)), 1.0, 0.0).astype(f32)
            d_decay = d_decay + hdot(ones, R.GS[level * tok : (level + 1) * tok])
        d_pre = d_decay / normalizer * lax.logistic(-R.PRE[...])
        src3 = R.AST3
        src3[:, :, width:] = jnp.zeros((nh, qrows, 128), bf16)
        d_low_part = hdot_t(d_pre, wf_r[:, fcols]).astype(bf16)
        for k in range(nh):
            src3[k, :, width : width + rank] = d_low_part[k * qrows : (k + 1) * qrows]
        ar_fill(3, dot_t(R.DP[0:tok], R.WA[...]))
        ar_start(3)
        R.SMALL[...] = jnp.zeros((mrows, kc), f32)
        R.SMALL[0:rank] = hdot_rows(R.LOW[...], d_pre)
        R.SMALL[rank : rank + 1] = jnp.sum(d_pre, axis=0, keepdims=True)
        for k in range(grow):
            R.SMALL[rank + 1 + k : rank + 2 + k] = group_row[:, k * kc : (k + 1) * kc]

        def all_pair(sems, src, dst, k, peer):
            return remote(
                src, dst, sems.at[0, k], sems.at[1, k], {SEQ: peer // nd, DP: lax.rem(peer, nd)}
            )

        for k in range(1, n * nd):
            peer = lax.rem(flat + k, n * nd)
            copy = all_pair(S.small, R.SMALL, R.SMALLL.at[flat], k, peer)
            copy.start()
            late.append(copy.wait_send)

        r_relay(1)
        act_wait(7, R.DYO, R.DY2.at[low_rows])
        act_wait(2, R.ZZ.at[top], R.ZZ.at[low_rows])
        R.RO[...] = dot_rows(R.ZZ[...], R.DY2[...]).astype(bf16)
        act_wait(0, R.XNO, R.XN2.at[low_rows])
        act_wait(8, R.DP.at[top], R.DP.at[low_rows])
        R.RA[...] = dot_rows(R.XN2[...], R.DP[...]).astype(bf16)
        for p in (3, 4):
            r_start(p, 0)
            r_start(p, 1)
        ar_mid(3)
        r_relay(2)
        ar_end(2)
        R.BOUT[...] = R.HRES[...] + ar_value(2)
        put_local(8, R.BOUT, bout_h)
        small = R.SMALL[...]
        for k in range(1, n * nd):
            came = lax.rem(flat + n * nd - k, n * nd)
            all_pair(S.small, R.SMALLL.at[came], R.SMALLL.at[came], k, came).wait_recv()
            small = small + R.SMALLL[came]
        R.SMH[...] = small
        R.SMHL[hh] = small
        for k in range(1, nh):
            to = lax.rem(hh + k, nh)
            copy = remote(R.SMH, R.SMHL.at[hh], S.smh.at[0, k], S.smh.at[1, k], {HEAD: to})
            copy.start()
            late.append(copy.wait_send)
        ar_end(3)
        x = R.X[...]
        scale_one = lax.rsqrt(jnp.mean(x * x, axis=-1, keepdims=True) + epsilon)
        gain_first = R.SIDE[rank : rank + 1].astype(f32)
        d_low = jnp.concatenate([R.ASM3[k, :, width : width + rank] for k in range(nh)], axis=0)
        d_xn = ar_value(3) + product(d_low, R.SIDE[0:rank])
        terms, d_norm = norm_back(x, scale_one, gain_first, d_xn)
        gain_one_grad = jnp.sum(terms, axis=0, keepdims=True)
        R.GIN[...] = R.DRES[...] + d_norm
        put_local(9, R.GIN, gin_h)
        low_grad = dot_rows(d_low, R.XN[...])
        R.TALL[...] = jnp.zeros((n, trows, shard), f32)
        for z in range(n):
            cols = slice(z * shard, (z + 1) * shard)
            R.TALL[z, 0:rank] = low_grad[:, cols]
            R.TALL[z, rank : rank + 1] = gain_one_grad[:, cols]
            R.TALL[z, rank + 1 : rank + 2] = gain_two_grad[:, cols]
        for k in range(1, n * nd):
            peer = lax.rem(flat + k, n * nd)
            copy = all_pair(S.tall, R.TALL.at[peer // nd], R.TALLL.at[flat], k, peer)
            copy.start()
            late.append(copy.wait_send)
        for p in range(3):
            r_close(p)
            put(p)
        r_relay(3)
        r_relay(4)
        tall = R.TALL[me]
        for k in range(1, n * nd):
            came = lax.rem(flat + n * nd - k, n * nd)
            all_pair(S.tall, R.TALLL.at[came], R.TALLL.at[came], k, came).wait_recv()
            tall = tall + R.TALLL[came]
        low_o[...] = tall[0:rank]
        again_o[...] = tall[rank : rank + 1]
        mgain_o[...] = tall[rank + 1 : rank + 2]
        for k in range(1, nh):
            came = lax.rem(hh + nh - k, nh)
            remote(R.SMHL.at[came], R.SMHL.at[came], S.smh.at[0, k], S.smh.at[1, k], {HEAD: came}).wait_recv()
        group = jnp.zeros((1, vc), f32)
        for h in range(nh):
            forget_o[:, h * kc : (h + 1) * kc] = R.SMHL[h, 0:rank]
            bias_o[:, h * kc : (h + 1) * kc] = R.SMHL[h, rank : rank + 1]
            group = group + jnp.concatenate(
                [R.SMHL[h, rank + 1 + k : rank + 2 + k] for k in range(grow)], axis=1
            )
        group_o[...] = group
        r_close(3)
        put(3)
        r_close(4)
        for i in range(4, 8):
            put(i)
        for wait in late:
            wait()

    return pl.pallas_call(
        kernel,
        out_shape=out_shape,
        in_specs=in_specs,
        out_specs=out_specs,
        scratch_shapes=scratch,
        compiler_params=pltpu.CompilerParams(
            collective_id=0, has_side_effects=True, vmem_limit_bytes=60 * 2**20
        ),
        name="fused_layer",
    )(*args)


def hand_over(arrays):
    count = len(arrays)

    def kernel(*refs):
        ins, outs, held = refs[:count], refs[count : 2 * count], refs[2 * count : 3 * count]
        sems = refs[3 * count]
        taken = [pltpu.make_async_copy(a, b, sems.at[0, i]) for i, (a, b) in enumerate(zip(ins, held))]
        given = [pltpu.make_async_copy(a, b, sems.at[1, i]) for i, (a, b) in enumerate(zip(held, outs))]
        for copy in taken:
            copy.start()
        for first, second in zip(taken, given):
            first.wait()
            second.start()
        for copy in given:
            copy.wait()

    anys = pl.BlockSpec(memory_space=pl.ANY)
    return pl.pallas_call(
        kernel,
        out_shape=[jax.ShapeDtypeStruct(a.shape, a.dtype) for a in arrays],
        in_specs=[anys] * count,
        out_specs=[anys] * count,
        scratch_shapes=[pltpu.VMEM(a.shape, a.dtype) for a in arrays] + [pltpu.SemaphoreType.DMA((2, count))],
        compiler_params=pltpu.CompilerParams(vmem_limit_bytes=16 * 2**20),
        name="hand_over",
    )(*arrays)


def one_kernel(
    x_in, cotangent, attn_gain, w_query, w_key, w_value, w_outgate, w_lowrank, w_forget, forget_bias,
    group_gain, w_output, mlp_gain, w_gate, w_up, w_down,
):
    n, nh, nd = lax.axis_size("seq"), lax.axis_size("head"), lax.axis_size("dp")
    _, tok, width = x_in.shape
    shard, rank = w_lowrank.shape
    kc, vc, hid = w_query.shape[1], w_value.shape[1], w_gate.shape[1]
    side = jnp.concatenate(
        (w_lowrank.T, attn_gain[None, :], mlp_gain[None, :], jnp.zeros((rank - 2, shard), jnp.bfloat16)), axis=0
    )
    outs = fused_layer(
        (n, nh, nd),
        (tok, width, shard, kc, vc, hid, rank),
        (
            x_in.reshape(tok, width),
            cotangent.reshape(tok, width),
            side,
            w_query,
            w_key,
            w_value,
            w_outgate,
            w_forget,
            forget_bias[None, :],
            group_gain[None, :],
            w_output,
            w_gate.T,
            w_up.T,
            w_down,
        ),
    )
    (result, grad_in, gq, gk, gv, gog, gwo, gg, gu, gd, glow, gain1, gain2, gforget, gbias, ggroup) = hand_over(outs)
    return (
        result[None],
        grad_in[None],
        gain1[0],
        gq,
        gk,
        gv,
        gog,
        glow.T,
        gforget,
        gbias[0],
        ggroup[0],
        gwo,
        gain2[0],
        gg.T,
        gu.T,
        gd,
    )


def fits_one_kernel(x_in, w_query, w_lowrank, w_value, w_gate):
    seqs, tok, _ = x_in.shape
    shard, rank = w_lowrank.shape
    n_head, n_dp = lax.axis_size("head"), lax.axis_size("dp")
    return (
        seqs == 1
        and n_dp == 2
        and lax.axis_size("seq") in (2, 3, 4)
        and tok & (tok - 1) == 0
        and tok % (16 * n_head) == 0
        and shard % 256 == 0
        and w_query.shape[1] == DK
        and w_value.shape[1] == DV
        and w_gate.shape[1] % 32 == 0
        and rank % 16 == 0
    )


def per_device(*args):
    x_in, w_query, w_value, w_lowrank, w_gate = args[0], args[3], args[5], args[7], args[13]
    if fits_one_kernel(x_in, w_query, w_lowrank, w_value, w_gate):
        return one_kernel(*args)
    return on_device(*args)


def solution(mesh):
    return jax.shard_map(
        per_device,
        mesh=mesh,
        in_specs=(
            P("dp", "seq", None),
            P("dp", "seq", None),
            P("seq"),
            P("seq", "head"),
            P("seq", "head"),
            P("seq", "head"),
            P("seq", "head"),
            P("seq", None),
            P(),
            P(),
            P(),
            P("head", "seq"),
            P("seq"),
            P("seq", "head"),
            P("seq", "head"),
            P("head", "seq"),
        ),
        out_specs=(
            P("dp", "seq", None),
            P("dp", "seq", None),
            P("seq"),
            P("seq", "head"),
            P("seq", "head"),
            P("seq", "head"),
            P("seq", "head"),
            P("seq", None),
            P(),
            P(),
            P(),
            P("head", "seq"),
            P("seq"),
            P("seq", "head"),
            P("seq", "head"),
            P("head", "seq"),
        ),
        check_vma=False,
    )
```

```python
from types import SimpleNamespace

import jax
import jax.numpy as jnp
from jax import lax
from jax.experimental import pallas as pl
from jax.experimental.pallas import tpu as pltpu
from jax.sharding import PartitionSpec as P

DK = 128
DV = 256
SPAN = 64
SEQ, HEAD, DP = "seq", "head", "dp"


epsilon = 1e-06
normalizer = 16.0
highest = lax.Precision.HIGHEST


def exchange(items, cid):
    groups = []
    for kind, axis, _ in items:
        for name in axis if kind in ("wg", "rs") else (axis,):
            if name not in groups:
                groups.append(name)
    names = []
    for group in groups:
        for name in group if isinstance(group, tuple) else (group,):
            if name not in names:
                names.append(name)
    size = {name: lax.axis_size(name) for name in names}
    for group in groups:
        if isinstance(group, tuple):
            size[group] = size[group[0]] * size[group[1]]
    out_shape, scratch = [], []
    dma = pltpu.SemaphoreType.DMA
    for kind, axis, arr in items:
        if kind in ("wg", "rs"):
            n, m = size[axis[0]], size[axis[1]]
            scratch += [dma((2, 2, n)), dma((2, 2, n, m))]
            if kind == "wg":
                out_shape.append(jax.ShapeDtypeStruct((n,) + arr.shape, arr.dtype))
                scratch.append(dma)
            else:
                out_shape.append(jax.ShapeDtypeStruct((m,) + arr.shape[1:], jnp.float32))
                scratch.append(pltpu.VMEM((2,) + arr.shape, arr.dtype))
                scratch.append(pltpu.VMEM((2,) + arr.shape, arr.dtype))
            continue
        n = size[axis]
        scratch.append(dma((2, n)))
        if kind == "ar":
            out_shape.append(jax.ShapeDtypeStruct(arr.shape, arr.dtype))
            scratch += [dma((2, n)), pltpu.VMEM(arr.shape, arr.dtype)]
        else:
            inner = arr.shape if kind == "ag" else arr.shape[1:]
            out_shape.append(jax.ShapeDtypeStruct((n,) + inner, arr.dtype))
            scratch.append(dma)

    def kernel(*refs):
        count = len(items)
        ins, outs, rest = refs[:count], refs[count : 2 * count], list(refs[2 * count :])
        me = {name: lax.axis_index(name) for name in names}
        for group in groups:
            if isinstance(group, tuple):
                me[group] = me[group[0]] * size[group[1]] + me[group[1]]

        def device(group, place):
            if isinstance(group, tuple):
                return {
                    group[0]: place // size[group[1]],
                    group[1]: lax.rem(place, size[group[1]]),
                }
            return {group: place}

        barrier = pltpu.get_barrier_semaphore()
        for group in groups:
            for k in range(1, size[group]):
                pl.semaphore_signal(
                    barrier,
                    inc=1,
                    device_id=device(group, lax.rem(me[group] + k, size[group])),
                    device_id_type=pl.DeviceIdType.MESH,
                )
        pl.semaphore_wait(barrier, sum(size[group] - 1 for group in groups))

        def remote(source, target, send, recv, group, place):
            return pltpu.make_async_remote_copy(
                src_ref=source,
                dst_ref=target,
                send_sem=send,
                recv_sem=recv,
                device_id=device(group, place),
                device_id_type=pl.DeviceIdType.MESH,
            )

        waits, chains, sums = [], [], []

        def chain_gather(src, dst, sems, sems_two, local, axis, arr):
            name, other = axis
            n, here, m, place = size[name], me[name], size[other], me[other]
            part = arr.shape[0] // m
            rows = pl.ds(pl.multiple_of(place * part, part), part)
            own = pltpu.make_async_copy(src, dst.at[here], local)
            own.start()
            waits.append(own.wait)

            def hop(way, step, source, index):
                to = here + 1 if way == 0 else here - 1
                return remote(
                    source,
                    dst.at[index, rows],
                    sems.at[way, 0, step],
                    sems.at[way, 1, step],
                    name,
                    to,
                )

            def guarded(ok, call):
                waits.append(lambda: pl.when(ok)(call))

            open_ends = (here < n - 1, here > 0)
            for way in range(2):
                @pl.when(open_ends[way])
                def _():
                    hop(way, 0, src.at[rows], here).start()

                guarded(
                    open_ends[way],
                    lambda way=way: hop(way, 0, src.at[rows], here).wait_send(),
                )

            def advance(step):
                for way in range(2):
                    came = here - 1 - step if way == 0 else here + 1 + step
                    ok = came >= 0 if way == 0 else came < n
                    on = jnp.logical_and(ok, open_ends[way])

                    def partners(way=way, came=came):
                        for j in range(1, m):
                            to = lax.rem(place + j, m)
                            whose = lax.rem(place + m - j, m)
                            piece = dst.at[came, rows]
                            theirs = dst.at[came, pl.ds(pl.multiple_of(whose * part, part), part)]
                            send, recv = sems_two.at[way, 0, step, j], sems_two.at[way, 1, step, j]
                            yield (
                                remote(piece, piece, send, recv, other, to),
                                remote(theirs, theirs, send, recv, other, to),
                            )

                    @pl.when(ok)
                    def _():
                        hop(way, step, dst.at[came, rows], came).wait_recv()

                    if step + 1 < n - 1:
                        @pl.when(on)
                        def _():
                            hop(way, step + 1, dst.at[came, rows], came).start()

                        guarded(
                            on,
                            lambda way=way, came=came: hop(
                                way, step + 1, dst.at[came, rows], came
                            ).wait_send(),
                        )

                    @pl.when(ok)
                    def _():
                        for copy, _ in partners():
                            copy.start()

                    def finish(partners=partners):
                        for copy, arrival in partners():
                            copy.wait_send()
                            arrival.wait_recv()

                    guarded(ok, finish)

            chains.append((n - 1, advance, lambda: None))

        def chain_sum(src, dst, sems, sems_two, land, held, axis, arr):
            name, other = axis
            n, here, m, place = size[name], me[name], size[other], me[other]
            tall = 16 if arr.shape[1] % 16 == 0 else arr.shape[1]
            turns = arr.shape[1] // tall

            def by_rows(call):
                def one(turn, carry):
                    call(pl.ds(pl.multiple_of(turn * tall, tall), tall))
                    return carry

                lax.fori_loop(0, turns, one, 0)

            def hop(way, step, source, index):
                to = here + 1 if way == 0 else here - 1
                return remote(
                    source,
                    land.at[way, index],
                    sems.at[way, 0, step],
                    sems.at[way, 1, step],
                    name,
                    to,
                )

            def guarded(ok, call):
                waits.append(lambda: pl.when(ok)(call))

            firsts = (here == 0, here == n - 1)

            def advance(step):
                for way in range(2):
                    goal = n - 1 - step if way == 0 else step
                    passing = here < goal if way == 0 else here > goal
                    inner = jnp.logical_and(passing, jnp.logical_not(firsts[way]))
                    first = jnp.logical_and(passing, firsts[way])

                    @pl.when(first)
                    def _():
                        if step > 0:
                            before = goal + 1 if way == 0 else goal - 1
                            hop(way, step - 1, src.at[before], before).wait_send()
                        hop(way, step, src.at[goal], goal).start()

                    if step == n - 2:
                        guarded(
                            first,
                            lambda way=way, goal=goal: hop(
                                way, step, src.at[goal], goal
                            ).wait_send(),
                        )

                    @pl.when(inner)
                    def _():
                        hop(way, step, land.at[way, goal], goal).wait_recv()

                        def add(rows):
                            held[way, goal, rows] = (
                                land[way, goal, rows].astype(jnp.float32)
                                + src[goal, rows].astype(jnp.float32)
                            ).astype(held.dtype)

                        by_rows(add)
                        hop(way, step, held.at[way, goal], goal).start()

                    guarded(
                        inner,
                        lambda way=way, goal=goal: hop(
                            way, step, held.at[way, goal], goal
                        ).wait_send(),
                    )

            def partners():
                for j in range(1, m):
                    to = lax.rem(place + j, m)
                    whose = lax.rem(place + m - j, m)
                    send, recv = sems_two.at[0, 0, 0, j], sems_two.at[0, 1, 0, j]
                    yield (
                        remote(dst.at[place], dst.at[place], send, recv, other, to),
                        remote(dst.at[whose], dst.at[whose], send, recv, other, to),
                    )

            def close():
                def start(rows):
                    dst[place, rows] = src[here, rows].astype(jnp.float32)

                by_rows(start)
                for way in range(2):
                    step = n - 1 - here if way == 0 else here

                    @pl.when(jnp.logical_not(firsts[way]))
                    def _():
                        hop(way, step, land.at[way, here], here).wait_recv()

                        def add(rows):
                            dst[place, rows] = dst[place, rows] + land[way, here, rows].astype(
                                jnp.float32
                            )

                        by_rows(add)

                for copy, _ in partners():
                    copy.start()
                for copy, arrival in partners():
                    waits.append(copy.wait_send)
                    waits.append(arrival.wait_recv)

            chains.append((n, advance, close))

        for (kind, axis, arr), src, dst in zip(items, ins, outs):
            if kind in ("wg", "rs"):
                extra = [rest.pop(0) for _ in range(3 if kind == "wg" else 4)]
                (chain_gather if kind == "wg" else chain_sum)(src, dst, *extra, axis, arr)
                continue
            sems = rest.pop(0)
            n, here = size[axis], me[axis]
            if kind == "ar":
                sems_two, land = rest.pop(0), rest.pop(0)
                sent = []
                for k in range(1, n):
                    peer = lax.rem(here + k, n)
                    came = lax.rem(here + n - k, n)
                    pair = sems.at[0, k], sems.at[1, k]
                    copy = remote(src.at[peer], land.at[here], *pair, axis, peer)
                    copy.start()
                    sent.append((copy, remote(land.at[came], land.at[came], *pair, axis, peer)))
                sums.append((src, dst, land, sems_two, axis, n, here, sent))
                continue
            local = rest.pop(0)

            def piece(place):
                if kind == "ag":
                    return src
                if isinstance(axis, tuple):
                    return src.at[place // size[axis[1]]]
                return src.at[place]

            own = pltpu.make_async_copy(piece(here), dst.at[here], local)
            own.start()
            waits.append(own.wait)
            for k in range(1, n):
                peer = lax.rem(here + k, n)
                came = lax.rem(here + n - k, n)
                pair = sems.at[0, k], sems.at[1, k]
                copy = remote(piece(peer), dst.at[here], *pair, axis, peer)
                copy.start()
                waits.append(copy.wait_send)
                waits.append(remote(dst.at[came], dst.at[came], *pair, axis, peer).wait_recv)

        def finish_sums():
            for src, dst, land, sems_two, axis, n, here, sent in sums:
                total = src[here].astype(jnp.float32)
                for k, (copy, arrival) in enumerate(sent, 1):
                    arrival.wait_recv()
                    total = total + land[lax.rem(here + n - k, n)].astype(jnp.float32)
                dst[here] = total.astype(dst.dtype)
                for k in range(1, n):
                    peer = lax.rem(here + k, n)
                    came = lax.rem(here + n - k, n)
                    pair = sems_two.at[0, k], sems_two.at[1, k]
                    copy = remote(dst.at[here], dst.at[here], *pair, axis, peer)
                    copy.start()
                    waits.append(copy.wait_send)
                    waits.append(
                        remote(dst.at[came], dst.at[came], *pair, axis, peer).wait_recv
                    )
                for copy, _ in sent:
                    waits.append(copy.wait_send)

        steps = max([entry[0] for entry in chains], default=0)
        for step in range(steps):
            if step == 1:
                finish_sums()
            for last, advance, _ in chains:
                if step < last:
                    advance(step)
        if steps < 2:
            finish_sums()
        for _, _, close in chains:
            close()
        for wait in waits:
            wait()

    def room(shape, dtype):
        item = jnp.dtype(dtype).itemsize
        lead = 1
        for extent in shape[:-2]:
            lead *= extent
        tile = 32 // item
        return lead * (-(-shape[-2] // tile) * tile) * (-(-shape[-1] // 128) * 128) * item

    total = sum(room(item[2].shape, item[2].dtype) for item in items)
    total += sum(room(shape.shape, shape.dtype) for shape in out_shape)
    for kind, _, arr in items:
        total += room(arr.shape, arr.dtype) * {"ar": 3, "rs": 4}.get(kind, 0)
    limit = min(60 * 2**20, total + total // 8 + 2 * 2**20)
    vmem = pl.BlockSpec(memory_space=pltpu.VMEM)
    return pl.pallas_call(
        kernel,
        out_shape=out_shape,
        in_specs=[vmem] * len(items),
        out_specs=[vmem] * len(items),
        scratch_shapes=scratch,
        compiler_params=pltpu.CompilerParams(
            collective_id=cid, has_side_effects=True, vmem_limit_bytes=limit
        ),
    )(*[item[2] for item in items])


def dot_t(left, right):
    return lax.dot_general(
        left, right, (((1,), (1,)), ((), ())), preferred_element_type=jnp.float32
    )


def dot_rows(left, right):
    return lax.dot_general(
        left, right, (((0,), (0,)), ((), ())), preferred_element_type=jnp.float32
    )


def product(left, right):
    return jnp.dot(left, right, preferred_element_type=jnp.float32)


def rms_rows(inputs):
    return lax.rsqrt(jnp.mean(inputs * inputs, axis=-1, keepdims=True) + epsilon)


def norm_back(inputs, scale, gain, grad):
    scaled = gain * grad
    gain_terms = grad * inputs * scale
    input_grad = scale * scaled - inputs * scale**3 * jnp.mean(
        scaled * inputs, axis=-1, keepdims=True
    )
    return (gain_terms, input_grad)


def mixer_block(queries, keys_in, values_in, log_decay, start_state):
    block_len = min(SPAN, queries.shape[0])
    blocks = queries.shape[0] // block_len

    def cut(array):
        return array.reshape(blocks, block_len, array.shape[-1])

    lower = jnp.tril(jnp.ones((block_len, block_len), jnp.float32))

    def block_step(carried, pieces):
        query_blk, key_blk, value_blk, decay_blk = pieces
        running = jnp.cumsum(decay_blk, axis=0)
        from_state = jnp.dot(query_blk * jnp.exp(running), carried, precision=highest)
        spread = (
            jnp.exp(jnp.minimum(running[:, None, :] - running[None, :, :], 0.0)) * lower[:, :, None]
        )
        scores = jnp.einsum("id,jd,ijd->ij", query_blk, key_blk, spread, precision=highest)
        inside = jnp.dot(scores, value_blk, precision=highest)
        ending = running[-1]
        weighted = key_blk * jnp.exp(ending[None, :] - running)
        carried = jnp.exp(ending)[:, None] * carried + jnp.dot(
            weighted.T, value_blk, precision=highest
        )
        return (carried, from_state + inside)

    final_state, outputs = lax.scan(
        jax.checkpoint(block_step),
        start_state,
        (cut(queries), cut(keys_in), cut(values_in), cut(log_decay)),
    )
    return (outputs.reshape(queries.shape[0], values_in.shape[-1]), final_state)


def on_device(
    x_in,
    cotangent,
    attn_gain,
    w_query,
    w_key,
    w_value,
    w_outgate,
    w_lowrank,
    w_forget,
    forget_bias,
    group_gain,
    w_output,
    mlp_gain,
    w_gate,
    w_up,
    w_down,
):
    seqs_here, tok_here, width = x_in.shape
    total_rows = seqs_here * tok_here
    bf16, f32 = jnp.bfloat16, jnp.float32
    n_seq, n_head, n_dp = lax.axis_size("seq"), lax.axis_size("head"), lax.axis_size("dp")
    seq_pos, head_pos = lax.axis_index("seq"), lax.axis_index("head")
    shard_rows = w_query.shape[0]
    part_rows = shard_rows // n_dp
    key_cols, val_cols, hidden = w_query.shape[1], w_value.shape[1], w_gate.shape[1]
    rank = w_lowrank.shape[1]
    heads_here = key_cols // DK
    head_scale = DK ** (-0.5)
    side = -(-(rank + 2) // 128) * 128
    packed = jnp.concatenate(
        (
            w_query,
            w_key,
            w_value,
            w_outgate,
            w_lowrank,
            attn_gain[:, None],
            mlp_gain[:, None],
            jnp.zeros((shard_rows, side - rank - 2), bf16),
            w_output.T,
        ),
        axis=1,
    )
    packed_mlp = jnp.concatenate((w_gate, w_up, w_down.T), axis=1)
    (weights,) = exchange([("wg", ("seq", "dp"), packed)], 0)
    weights = weights.reshape(width, -1)
    attn_cols = 2 * key_cols + 2 * val_cols
    w_attn = weights[:, :attn_cols]
    w_low = weights[:, attn_cols : attn_cols + side]
    wl_full = w_low[:, :rank]
    gain_first = w_low[:, rank].astype(f32)
    gain_second = w_low[:, rank + 1].astype(f32)
    at = attn_cols + side
    wo_t = weights[:, at : at + val_cols]
    forget_cols = lax.dynamic_slice_in_dim(w_forget, head_pos * key_cols, key_cols, 1)
    bias_cols = lax.dynamic_slice_in_dim(forget_bias, head_pos * key_cols, key_cols, 0)

    def heads_of(array, size):
        return array.reshape(seqs_here, tok_here, heads_here, size).transpose(0, 2, 1, 3)

    def rows_of(array):
        return array.transpose(0, 2, 1, 3).reshape(total_rows, -1)

    def spread_head(array):
        return array.astype(bf16).reshape(n_head, array.shape[0] // n_head, array.shape[1])

    def by_part(array):
        array = array.reshape(total_rows, n_seq, n_dp, part_rows)
        return array.transpose(2, 0, 1, 3).reshape(n_dp, total_rows, n_seq * part_rows)

    def all_rows(array):
        return array.reshape(n_dp * total_rows, -1)

    def grad_of(left, right):
        return dot_rows(all_rows(left), all_rows(right)).astype(bf16)

    flat_in = x_in.reshape(total_rows, width)
    flat_cot = cotangent.reshape(total_rows, width)
    scale_one = rms_rows(flat_in)
    normed_in = (flat_in * scale_one * gain_first).astype(bf16)
    proj = product(normed_in, w_attn)
    q_rows = proj[:, :key_cols]
    k_rows = proj[:, key_cols : 2 * key_cols]
    v_rows = proj[:, 2 * key_cols : 2 * key_cols + val_cols]
    og_rows = proj[:, 2 * key_cols + val_cols :]
    low_rank = product(normed_in, wl_full)
    pre_gate = jnp.dot(low_rank, forget_cols, precision=highest) + bias_cols
    log_decay = jax.nn.log_sigmoid(pre_gate) / normalizer
    q_heads = heads_of(q_rows, DK)
    k_heads = heads_of(k_rows, DK)
    v_heads = heads_of(v_rows, DV)
    decay_heads = heads_of(log_decay, DK)
    running = jnp.cumsum(decay_heads, axis=2)
    ending = running[:, :, -1, :]
    decay_total = jnp.exp(ending)
    local_state = jnp.einsum(
        "shld,shlv->shdv",
        k_heads * jnp.exp(ending[:, :, None, :] - running),
        v_heads,
        precision=highest,
    )
    state_shape = local_state.shape
    states, decays = exchange(
        [
            ("ag", "seq", local_state.astype(bf16).reshape(-1, DV)),
            ("ag", "seq", jnp.broadcast_to(decay_total.reshape(1, -1), (8, decay_total.size))),
        ],
        1,
    )
    decays = decays[:, 0].reshape((n_seq,) + decay_total.shape)
    states = states.reshape((n_seq,) + state_shape)
    start_state = jnp.zeros(state_shape, f32)
    for j in range(n_seq - 1):
        start_state = jnp.where(
            j < seq_pos, decays[j][..., None] * start_state + states[j].astype(f32), start_state
        )

    def mixed(q_part, k_part, v_part, d_part):
        return jax.vmap(jax.vmap(mixer_block))(
            q_part * head_scale, k_part, v_part, d_part, start_state
        )

    (o_heads, end_state), pullback = jax.vjp(mixed, q_heads, k_heads, v_heads, decay_heads)
    gate_heads = heads_of(og_rows, DV)
    scale_three = rms_rows(o_heads)
    gated_norm = o_heads * scale_three * group_gain
    gate_sig = jax.nn.sigmoid(gate_heads)
    gate_act = gate_heads * gate_sig
    mixed_out = rows_of(gated_norm * gate_act).astype(bf16)
    mix_sum, weights_mlp = exchange(
        [
            ("ar", "head", spread_head(dot_t(mixed_out, wo_t))),
            ("wg", ("seq", "dp"), packed_mlp),
        ],
        2,
    )
    weights_mlp = weights_mlp.reshape(width, -1)
    w_gu = weights_mlp[:, : 2 * hidden]
    wdown_t = weights_mlp[:, 2 * hidden :]
    resid = flat_in + mix_sum.reshape(total_rows, width).astype(f32)
    scale_two = rms_rows(resid)
    normed_mid = (resid * scale_two * gain_second).astype(bf16)
    both = product(normed_mid, w_gu)
    gate_pre, up_pre = both[:, :hidden], both[:, hidden:]
    gate_sigma = jax.nn.sigmoid(gate_pre)
    gate_silu = gate_pre * gate_sigma
    mlp_hidden = (gate_silu * up_pre).astype(bf16)
    grad_out_b = flat_cot.astype(bf16)
    d_hidden = product(grad_out_b, wdown_t)
    d_gate_pre = (d_hidden * up_pre * gate_sigma * (1.0 + gate_pre * (1.0 - gate_sigma))).astype(
        bf16
    )
    d_up_pre = (d_hidden * gate_silu).astype(bf16)
    d_both = jnp.concatenate((d_gate_pre, d_up_pre), axis=1)
    sums, mid_two, out_two, both_two, hidden_two = exchange(
        [
            (
                "ar",
                "head",
                spread_head(
                    jnp.concatenate((dot_t(mlp_hidden, wdown_t), dot_t(d_both, w_gu)), axis=0)
                ),
            ),
            ("a2a", "dp", by_part(normed_mid)),
            ("a2a", "dp", by_part(grad_out_b)),
            ("ag", "dp", d_both),
            ("ag", "dp", mlp_hidden),
        ],
        3,
    )
    sums = sums.reshape(2, total_rows, width).astype(f32)
    result = resid + sums[0]
    d_normed_mid = sums[1]
    gain_terms, d_resid_norm = norm_back(resid, scale_two, gain_second, d_normed_mid)
    d_gain_two = jnp.sum(gain_terms, axis=0)
    d_resid = flat_cot + d_resid_norm
    d_resid_b = d_resid.astype(bf16)
    d_mixed = heads_of(product(d_resid_b, wo_t), DV)
    d_norm_out = d_mixed * gate_act
    d_gate_heads = d_mixed * gated_norm * gate_sig * (1.0 + gate_heads * (1.0 - gate_sig))
    d_group = jnp.sum(d_norm_out * o_heads * scale_three, axis=(0, 1, 2))
    group_terms, d_o_heads = norm_back(o_heads, scale_three, group_gain, d_norm_out)
    state_grad = jnp.einsum(
        "shld,shlv->shdv", q_heads * head_scale * jnp.exp(running), d_o_heads, precision=highest
    )
    grads_in, mixed_two, resid_two = exchange(
        [
            ("ag", "seq", state_grad.astype(bf16).reshape(-1, DV)),
            ("ag", "dp", mixed_out),
            ("a2a", "dp", by_part(d_resid_b)),
        ],
        4,
    )
    grads_late = jnp.concatenate(
        (
            grad_of(resid_two, mixed_two),
            grad_of(mid_two, both_two),
            grad_of(out_two, hidden_two),
        ),
        axis=1,
    ).reshape(n_seq, part_rows, -1)
    grads_in = grads_in.reshape((n_seq,) + state_shape)
    later_grad = jnp.zeros(state_shape, f32)
    for j in range(n_seq - 1, 0, -1):
        later_grad = jnp.where(
            j > seq_pos, decays[j][..., None] * later_grad + grads_in[j].astype(f32), later_grad
        )
    d_q, d_k, d_v, d_decay = pullback((d_o_heads, later_grad))
    d_pre = rows_of(d_decay) / normalizer * jax.nn.sigmoid(-pre_gate)
    d_bias = jnp.sum(d_pre, axis=0)
    d_forget = jnp.dot(low_rank.T, d_pre, precision=highest)
    d_low_part = jnp.dot(d_pre, forget_cols.T, precision=highest)
    d_proj = jnp.concatenate(
        (
            rows_of(d_q).astype(bf16),
            rows_of(d_k).astype(bf16),
            rows_of(d_v).astype(bf16),
            rows_of(d_gate_heads).astype(bf16),
        ),
        axis=1,
    )
    d_in_part = jnp.concatenate(
        (dot_t(d_proj, w_attn), d_low_part, jnp.zeros((total_rows, side - rank), f32)), axis=1
    )
    group_rows = d_group.reshape(1, DV)
    if DV < key_cols:
        group_rows = jnp.pad(group_rows, ((0, 0), (0, key_cols - DV)))
    if DV > key_cols:
        group_rows = group_rows.reshape(-1, key_cols)
    used = rank + 1 + group_rows.shape[0]
    small = jnp.concatenate(
        (
            d_forget,
            d_bias[None, :],
            group_rows,
            jnp.zeros((-used % 8, key_cols), f32),
        ),
        axis=0,
    )
    grads_late, in_sum, small_all, in_two, proj_two = exchange(
        [
            ("rs", ("seq", "dp"), grads_late),
            ("ar", "head", spread_head(d_in_part)),
            ("ag", ("seq", "dp"), small),
            ("a2a", "dp", by_part(normed_in)),
            ("ag", "dp", d_proj),
        ],
        5,
    )
    in_sum = in_sum.reshape(total_rows, width + side)
    d_low_b = in_sum[:, width : width + rank]
    d_normed_in = in_sum[:, :width].astype(f32) + dot_t(d_low_b, wl_full)
    first_terms, d_in_norm = norm_back(flat_in, scale_one, gain_first, d_normed_in)
    d_gain_one = jnp.sum(first_terms, axis=0)
    grad_in = d_resid + d_in_norm

    grads_attn = grad_of(in_two, proj_two).reshape(n_seq, part_rows, -1)
    tall = jnp.concatenate(
        (
            dot_rows(d_low_b, normed_in),
            d_gain_one[None, :],
            d_gain_two[None, :],
            jnp.zeros((-(rank + 2) % 8, width), f32),
        ),
        axis=0,
    )
    tall = tall.reshape(-1, n_seq, shard_rows).transpose(1, 0, 2)
    grads_attn, tall, small = exchange(
        [
            ("rs", ("seq", "dp"), grads_attn),
            ("a2a", ("seq", "dp"), tall),
            ("ag", "head", jnp.sum(small_all, axis=0)),
        ],
        6,
    )
    grads_attn = grads_attn.reshape(shard_rows, -1)
    grads_late = grads_late.reshape(shard_rows, -1)
    tall = jnp.sum(tall, axis=0)
    s_forget = small[:, :rank].transpose(1, 0, 2).reshape(rank, -1)
    s_bias = small[:, rank].reshape(-1)
    s_group = jnp.sum(small[:, rank + 1 : used], axis=0).reshape(-1)[:DV]
    s_query, s_key, s_value, s_outgate = jnp.split(
        grads_attn, [key_cols, 2 * key_cols, 2 * key_cols + val_cols], axis=1
    )
    s_output, s_gate, s_up, s_down = jnp.split(
        grads_late, [val_cols, val_cols + hidden, val_cols + 2 * hidden], axis=1
    )
    return (
        result.reshape(seqs_here, tok_here, width),
        grad_in.reshape(seqs_here, tok_here, width),
        tall[rank],
        s_query,
        s_key,
        s_value,
        s_outgate,
        tall[:rank].T,
        s_forget,
        s_bias,
        s_group,
        s_output.T,
        tall[rank + 1],
        s_gate,
        s_up,
        s_down.T,
    )


def fused_layer(axes, dims, args):
    n, nh, nd = axes
    tok, width, shard, kc, vc, hid, rank = dims
    bf16, f32 = jnp.bfloat16, jnp.float32
    half = shard // 2
    nhalf = n * half
    acols = 2 * kc + 2 * vc
    cuts = ((0, kc), (kc, kc), (2 * kc, vc), (2 * kc + vc, vc))
    qrows = tok // nh
    hhid = hid // 2
    hkv = vc // 2
    scale = DK ** (-0.5)
    levels = []
    size = tok // 2
    while size:
        levels.append(size)
        size //= 2
    nl = len(levels) + 2
    srows = rank * 2
    trows = -(-(rank + 2) // 8) * 8
    grow = vc // kc
    mrows = -(-(rank + 1 + grow) // 8) * 8
    dma = pltpu.SemaphoreType.DMA
    n_gather = 6
    n_sum = 5
    n_ar = 4

    out_shape = [
        jax.ShapeDtypeStruct((tok, width), f32),
        jax.ShapeDtypeStruct((tok, width), f32),
        jax.ShapeDtypeStruct((shard, kc), f32),
        jax.ShapeDtypeStruct((shard, kc), f32),
        jax.ShapeDtypeStruct((shard, vc), f32),
        jax.ShapeDtypeStruct((shard, vc), f32),
        jax.ShapeDtypeStruct((vc, shard), f32),
        jax.ShapeDtypeStruct((hid, shard), f32),
        jax.ShapeDtypeStruct((hid, shard), f32),
        jax.ShapeDtypeStruct((hid, shard), f32),
        jax.ShapeDtypeStruct((rank, shard), f32),
        jax.ShapeDtypeStruct((1, shard), f32),
        jax.ShapeDtypeStruct((1, shard), f32),
        jax.ShapeDtypeStruct((rank, nh * kc), f32),
        jax.ShapeDtypeStruct((1, nh * kc), f32),
        jax.ShapeDtypeStruct((1, vc), f32),
    ]
    anys = pl.BlockSpec(memory_space=pl.ANY)
    vmem = pl.BlockSpec(memory_space=pltpu.VMEM)
    out_specs = [anys] * 10 + [vmem] * 6
    in_specs = [anys] * 7 + [vmem] * 3 + [anys] * 4

    shapes = dict(
        X=((tok, width), f32),
        COT=((tok, width), f32),
        WA=((width, acols), bf16),
        SIDE=((srows, width), bf16),
        WO=((vc, width), bf16),
        WG=((hid, width), bf16),
        WU=((hid, width), bf16),
        WD=((hid, width), bf16),
        XS=((nl, tok, DK), f32),
        GS=((nl * tok, DK), f32),
        QKVO=((tok, acols), f32),
        PRE=((tok, kc), f32),
        LOW=((tok, rank), f32),
        AM=((tok, tok), f32),
        ST=((vc, DK), bf16),
        STL=((n, vc, DK), bf16),
        DEC=((8, DK), f32),
        DECL=((n, 8, DK), f32),
        S0=((vc, DK), f32),
        SG=((vc, DK), bf16),
        SGL=((n, vc, DK), bf16),
        LG=((vc, DK), f32),
        O=((tok, vc), f32),
        HRES=((tok, width), f32),
        HN=((tok, width), bf16),
        DRES=((tok, width), f32),
        XN=((tok, width), bf16),
        DMIX=((tok, vc), f32),
        AST0=((nh, qrows, width), bf16),
        ALD0=((nh, qrows, width), bf16),
        ASM0=((nh, qrows, width), bf16),
        AST1=((nh, qrows, width), bf16),
        ALD1=((nh, qrows, width), bf16),
        ASM1=((nh, qrows, width), bf16),
        AST2=((nh, qrows, width), bf16),
        ALD2=((nh, qrows, width), bf16),
        ASM2=((nh, qrows, width), bf16),
        AST3=((nh, qrows, width + 128), bf16),
        ALD3=((nh, qrows, width + 128), bf16),
        ASM3=((nh, qrows, width + 128), bf16),
        HN2=((2 * tok, nhalf), bf16),
        HNO=((tok, nhalf), bf16),
        GO2=((2 * tok, nhalf), bf16),
        GOO=((tok, nhalf), bf16),
        DY2=((2 * tok, nhalf), bf16),
        DYO=((tok, nhalf), bf16),
        XN2=((2 * tok, nhalf), bf16),
        XNO=((tok, nhalf), bf16),
        DA1=((2 * tok, hid), bf16),
        DA2=((2 * tok, hid), bf16),
        MM=((2 * tok, hid), bf16),
        ZZ=((2 * tok, vc), bf16),
        DP=((2 * tok, acols), bf16),
        RG=((hid, nhalf), bf16),
        RU=((hid, nhalf), bf16),
        RD=((hid, nhalf), bf16),
        RO=((vc, nhalf), bf16),
        RA=((nhalf, acols), bf16),
        LG_=((2, 3, hid, half), bf16),
        LU_=((2, 3, hid, half), bf16),
        LD_=((2, 3, hid, half), bf16),
        LO_=((2, 3, vc, half), bf16),
        LA_=((2, 3, half, acols), bf16),
        FG=((hid, half), f32),
        FU=((hid, half), f32),
        FD=((hid, half), f32),
        FO=((vc, half), f32),
        FA=((half, acols), f32),
        BOUT=((tok, width), f32),
        GIN=((tok, width), f32),
        TALL=((n, trows, shard), f32),
        TALLL=((n * nd, trows, shard), f32),
        SMALL=((mrows, kc), f32),
        SMALLL=((n * nd, mrows, kc), f32),
        SMH=((mrows, kc), f32),
        SMHL=((nh, mrows, kc), f32),
    )
    names = list(shapes)
    scratch = [pltpu.VMEM(*shapes[name]) for name in names]
    sem_shapes = dict(
        load=(12,),
        gat=(n_gather, 2, 2, n - 1),
        gtwo=(n_gather, 2, 2, n - 1),
        st=(2, n),
        dec=(2, n),
        sg=(2, n),
        ara=(n_ar, 2, nh),
        arb=(n_ar, 2, nh),
        act=(2, 9),
        rs=(n_sum, 2, 2, 3),
        outl=(12,),
        outr=(2, 8),
        tall=(2, n * nd),
        small=(2, n * nd),
        smh=(2, nh),
    )
    sem_names = list(sem_shapes)
    scratch += [dma(sem_shapes[name]) for name in sem_names]

    def kernel(*refs):
        (x_h, cot_h, side_h, wq_h, wk_h, wv_h, wog_h, wf_r, fb_r, gg_r, wo_h, wg_h, wu_h, wd_h) = refs[:14]
        outs = refs[14:30]
        (bout_h, gin_h, gq_h, gk_h, gv_h, gog_h, gwo_h, gg_h, gu_h, gd_h) = outs[:10]
        (low_o, again_o, mgain_o, forget_o, bias_o, group_o) = outs[10:]
        R = SimpleNamespace(**dict(zip(names, refs[30 : 30 + len(names)])))
        S = SimpleNamespace(**dict(zip(sem_names, refs[30 + len(names) :])))
        me, hh, dd = lax.axis_index(SEQ), lax.axis_index(HEAD), lax.axis_index(DP)
        other = 1 - dd
        mesh_id = pl.DeviceIdType.MESH

        def remote(src, dst, send, recv, to):
            return pltpu.make_async_remote_copy(
                src_ref=src, dst_ref=dst, send_sem=send, recv_sem=recv, device_id=to, device_id_type=mesh_id
            )

        def mult(value, by):
            return pl.multiple_of(value * by, by)

        def lanes_of(place):
            return pl.ds(mult(place, shard), shard)

        late = []

        rows_me = pl.ds(mult(me, shard), shard)
        loads = [
            (wq_h, R.WA.at[rows_me, 0:kc]),
            (wk_h, R.WA.at[rows_me, kc : 2 * kc]),
            (wv_h, R.WA.at[rows_me, 2 * kc : 2 * kc + vc]),
            (wog_h, R.WA.at[rows_me, 2 * kc + vc : acols]),
            (side_h, R.SIDE.at[:, lanes_of(me)]),
            (x_h, R.X),
            (wo_h, R.WO.at[:, lanes_of(me)]),
            (wg_h, R.WG.at[:, lanes_of(me)]),
            (wu_h, R.WU.at[:, lanes_of(me)]),
            (wd_h, R.WD.at[:, lanes_of(me)]),
            (cot_h, R.COT),
        ]
        loads = [pltpu.make_async_copy(a, b, S.load.at[i]) for i, (a, b) in enumerate(loads)]
        for copy in loads:
            copy.start()

        barrier = pltpu.get_barrier_semaphore()
        count = 0
        for k in range(1, nh):
            pl.semaphore_signal(barrier, inc=1, device_id={HEAD: lax.rem(hh + k, nh)}, device_id_type=mesh_id)
            count += 1
        flat = me * nd + dd
        for k in range(1, n * nd):
            peer = lax.rem(flat + k, n * nd)
            pl.semaphore_signal(
                barrier, inc=1, device_id={SEQ: peer // nd, DP: lax.rem(peer, nd)}, device_id_type=mesh_id
            )
            count += 1
        pl.semaphore_wait(barrier, count)

        def rows_view(ref, c, d):
            return ref.at[pl.ds(pl.multiple_of(c * shard + d * half, half), half)]

        def lane_view(rows):
            return lambda ref, c, d: ref.at[pl.ds(mult(d, rows), rows), lanes_of(c)]

        pieces = [
            (R.WA, rows_view),
            (R.SIDE, lane_view(rank)),
            (R.WO, lane_view(hkv)),
            (R.WG, lane_view(hhid)),
            (R.WU, lane_view(hhid)),
            (R.WD, lane_view(hhid)),
        ]
        open_ends = (me < n - 1, me > 0)

        def guarded(ok, call):
            late.append(lambda: pl.when(ok)(call))

        def g_hop(p, way, step, c):
            ref, view = pieces[p]
            v = view(ref, c, dd)
            return remote(v, v, S.gat.at[p, way, 0, step], S.gat.at[p, way, 1, step], {SEQ: me + 1 if way == 0 else me - 1})

        def g_pair(p, way, step, c, d):
            ref, view = pieces[p]
            v = view(ref, c, d)
            return remote(v, v, S.gtwo.at[p, way, 0, step], S.gtwo.at[p, way, 1, step], {DP: other})

        def d_send(p, way, dist):
            ref, view = pieces[p]
            v = view(ref, me, dd)
            to = me + dist if way == 0 else me - dist
            return remote(v, v, S.gat.at[p, way, 0, dist - 1], S.gat.at[p, way, 1, dist - 1], {SEQ: to})

        def reach(way, dist):
            return me + dist < n if way == 0 else me - dist >= 0

        def d_own(p):
            for dist in range(min(2, n - 1), 0, -1):
                for way in range(2):
                    ok = reach(way, dist)
                    pl.when(ok)(lambda way=way, dist=dist: d_send(p, way, dist).start())
                    guarded(ok, lambda way=way, dist=dist: d_send(p, way, dist).wait_send())

        def d_take(p, dist):
            if dist >= n:
                return
            for way in range(2):
                c, ok = came_of(way, dist - 1)
                pl.when(ok)(lambda way=way, c=c: g_hop(p, way, dist - 1, c).wait_recv())
                if dist == 2 and n > 3:
                    on = jnp.logical_and(ok, open_ends[way])
                    pl.when(on)(lambda way=way, c=c: g_hop(p, way, 2, c).start())
                    guarded(on, lambda way=way, c=c: g_hop(p, way, 2, c).wait_send())
                pl.when(ok)(lambda way=way, c=c: g_pair(p, way, dist - 1, c, dd).start())
                guarded(ok, lambda way=way, c=c: g_pair(p, way, dist - 1, c, dd).wait_send())

        def came_of(way, step):
            c = me - 1 - step if way == 0 else me + 1 + step
            return c, (c >= 0 if way == 0 else c < n)

        def g_own(p):
            for way in range(2):
                pl.when(open_ends[way])(lambda way=way: g_hop(p, way, 0, me).start())
                guarded(open_ends[way], lambda way=way: g_hop(p, way, 0, me).wait_send())

        def g_step(p, step):
            for way in range(2):
                c, ok = came_of(way, step)
                on = jnp.logical_and(ok, open_ends[way])
                pl.when(ok)(lambda way=way, c=c: g_hop(p, way, step, c).wait_recv())
                if step + 1 < n - 1:
                    pl.when(on)(lambda way=way, c=c: g_hop(p, way, step + 1, c).start())
                    guarded(on, lambda way=way, c=c: g_hop(p, way, step + 1, c).wait_send())
                pl.when(ok)(lambda way=way, c=c: g_pair(p, way, step, c, dd).start())
                guarded(ok, lambda way=way, c=c: g_pair(p, way, step, c, dd).wait_send())

        def g_end(p):
            for step in range(n - 1):
                for way in range(2):
                    c, ok = came_of(way, step)
                    pl.when(ok)(lambda way=way, c=c, step=step: g_pair(p, way, step, c, other).wait_recv())

        heads = (
            (R.AST0, R.ALD0, R.ASM0),
            (R.AST1, R.ALD1, R.ASM1),
            (R.AST2, R.ALD2, R.ASM2),
            (R.AST3, R.ALD3, R.ASM3),
        )

        def ar_refs(k):
            return heads[k]

        def ar_pair(k, sems, src, dst, j, to):
            return remote(src, dst, sems.at[k, 0, j], sems.at[k, 1, j], {HEAD: to})

        def ar_start(k):
            src, land, _ = ar_refs(k)
            for j in range(1, nh):
                to = lax.rem(hh + j, nh)
                copy = ar_pair(k, S.ara, src.at[to], land.at[hh], j, to)
                copy.start()
                late.append(copy.wait_send)

        def ar_mid(k):
            src, land, dst = ar_refs(k)
            total = src[hh].astype(f32)
            for j in range(1, nh):
                came = lax.rem(hh + nh - j, nh)
                ar_pair(k, S.ara, land.at[came], land.at[came], j, came).wait_recv()
                total = total + land[came].astype(f32)
            dst[hh] = total.astype(bf16)
            for j in range(1, nh):
                to = lax.rem(hh + j, nh)
                copy = ar_pair(k, S.arb, dst.at[hh], dst.at[hh], j, to)
                copy.start()
                late.append(copy.wait_send)

        def ar_end(k):
            dst = ar_refs(k)[2]
            for j in range(1, nh):
                came = lax.rem(hh + nh - j, nh)
                ar_pair(k, S.arb, dst.at[came], dst.at[came], j, came).wait_recv()

        def ar_fill(k, value):
            src = ar_refs(k)[0]
            for j in range(nh):
                src[j, :, : value.shape[1]] = value[j * qrows : (j + 1) * qrows].astype(bf16)

        def ar_value(k, cols=width):
            dst = ar_refs(k)[2]
            return jnp.concatenate([dst[j, :, :cols] for j in range(nh)], axis=0).astype(f32)

        def act_send(i, src, dst):
            copy = remote(src, dst, S.act.at[0, i], S.act.at[1, i], {DP: other})
            copy.start()
            late.append(copy.wait_send)

        def act_wait(i, src, dst):
            remote(src, dst, S.act.at[0, i], S.act.at[1, i], {DP: other}).wait_recv()

        top, low_rows = pl.ds(0, tok), pl.ds(tok, tok)

        def split(value, mine, theirs):
            for z in range(n):
                lo = value[:, z * shard : z * shard + half]
                hi = value[:, z * shard + half : (z + 1) * shard]
                first = dd == 0
                mine[0:tok, z * half : (z + 1) * half] = jnp.where(first, lo, hi)
                theirs[:, z * half : (z + 1) * half] = jnp.where(first, hi, lo)

        sums = [
            (R.RG, R.LG_, R.FG, True),
            (R.RU, R.LU_, R.FU, True),
            (R.RD, R.LD_, R.FD, True),
            (R.RO, R.LO_, R.FO, True),
            (R.RA, R.LA_, R.FA, False),
        ]

        def chunk(p, g):
            ref, kind = sums[p][0], sums[p][3]
            at = g * half if isinstance(g, int) else mult(g, half)
            if kind:
                return ref.at[:, pl.ds(at, half)]
            return ref.at[pl.ds(at, half)]

        def r_send(p, way, slot, src, to):
            return remote(
                src, sums[p][1].at[way, slot], S.rs.at[p, way, 0, slot], S.rs.at[p, way, 1, slot], {SEQ: to}
            )

        ends = (me == 0, me == n - 1)
        seconds = (me == 1, me == n - 2)

        def r_start(p, way):
            far = n - 1 if way == 0 else 0
            step = 1 if way == 0 else -1
            if n > 3:
                pl.when(ends[way])(lambda: r_send(p, way, 2, chunk(p, far), me + step).start())
                guarded(ends[way], lambda: r_send(p, way, 2, chunk(p, far), me + step).wait_send())
            for dist in range(min(2, n - 1), 0, -1):
                ok = reach(way, dist)
                if dist == 2 and n > 3:
                    ok = jnp.logical_and(ok, jnp.logical_not(seconds[way]))
                to = me + dist * step
                pl.when(ok)(lambda dist=dist, to=to: r_send(p, way, dist - 1, chunk(p, to), to).start())
                guarded(ok, lambda dist=dist, to=to: r_send(p, way, dist - 1, chunk(p, to), to).wait_send())

        def r_relay(p):
            land = sums[p][1]
            if n > 3:
                for way in range(2):
                    far = n - 1 if way == 0 else 0

                    @pl.when(seconds[way])
                    def _():
                        r_send(p, way, 2, land.at[way, 2], me).wait_recv()
                        land[way, 2] = (land[way, 2].astype(f32) + chunk(p, far)[...].astype(f32)).astype(bf16)
                        r_send(p, way, 1, land.at[way, 2], far).start()

                    guarded(seconds[way], lambda way=way, far=far: r_send(p, way, 1, land.at[way, 2], far).wait_send())

        def r_close(p):
            land, fin = sums[p][1], sums[p][2]
            fin[...] = chunk(p, me)[...].astype(f32)
            for dist in range(1, min(2, n - 1) + 1):
                for way in range(2):

                    @pl.when(reach(1 - way, dist))
                    def _():
                        r_send(p, way, dist - 1, land.at[way, dist - 1], me).wait_recv()
                        fin[...] = fin[...] + land[way, dist - 1].astype(f32)

        outputs = [
            (R.FG, gg_h, True),
            (R.FU, gu_h, True),
            (R.FD, gd_h, True),
            (R.FO, gwo_h, True),
        ] + [(R.FA.at[:, at : at + w], ref, False) for (at, w), ref in zip(cuts, (gq_h, gk_h, gv_h, gog_h))]

        def out_view(ref, kind, d):
            place = pl.ds(mult(d, half), half)
            return ref.at[:, place] if kind else ref.at[place]

        def put(i):
            src, ref, kind = outputs[i]
            view = out_view(ref, kind, dd)
            copy = pltpu.make_async_copy(src, view, S.outl.at[i])
            copy.start()
            late.append(copy.wait)
            copy = remote(src, view, S.outr.at[0, i], S.outr.at[1, i], {DP: other})
            copy.start()
            late.append(copy.wait_send)
            theirs = out_view(ref, kind, other)
            late.append(remote(theirs, theirs, S.outr.at[0, i], S.outr.at[1, i], {DP: other}).wait_recv)

        def put_local(i, src, ref):
            copy = pltpu.make_async_copy(src, ref, S.outl.at[i])
            copy.start()
            late.append(copy.wait)

        def hdot(a, b):
            return jnp.dot(a, b, precision=highest, preferred_element_type=f32)

        def hdot_t(a, b):
            return lax.dot_general(a, b, (((1,), (1,)), ((), ())), precision=highest, preferred_element_type=f32)

        def hdot_rows(a, b):
            return lax.dot_general(a, b, (((0,), (0,)), ((), ())), precision=highest, preferred_element_type=f32)

        def iota(axis):
            return lax.broadcasted_iota(jnp.int32, (tok, tok), axis)

        def span(level, i, t):
            if level == nl - 2:
                return t <= i
            if level == nl - 1:
                return t > i
            b = levels[level]
            r = (i & ~(2 * b - 1)) + (b - 1)
            upper = (i & b) != 0
            return jnp.logical_or(
                jnp.logical_and(upper, jnp.logical_and(t > r, t <= i)),
                jnp.logical_and(jnp.logical_not(upper), jnp.logical_and(t > i, t <= r)),
            )

        def mask_of(level):
            b = levels[level]
            i, j = iota(0), iota(1)
            same = (i & ~(2 * b - 1)) == (j & ~(2 * b - 1))
            return jnp.logical_and(same, jnp.logical_and((i & b) != 0, (j & b) == 0))

        def upper_rows(level):
            return (lax.broadcasted_iota(jnp.int32, (tok, DK), 0) & levels[level]) != 0

        for copy in loads[:5]:
            copy.wait()
        g_own(1)
        g_own(0)
        loads[5].wait()
        x = R.X[...]
        scale_one = lax.rsqrt(jnp.mean(x * x, axis=-1, keepdims=True) + epsilon)
        for step in range(n - 1):
            g_step(1, step)
            g_step(0, step)
        for copy in loads[6:]:
            copy.wait()
        d_own(2)
        d_own(3)
        g_end(1)
        gain_first = R.SIDE[rank : rank + 1].astype(f32)
        normed = (x * scale_one * gain_first).astype(bf16)
        R.XN[...] = normed
        low = dot_t(normed, R.SIDE[0:rank])
        R.LOW[...] = low
        fcols = pl.ds(mult(hh, kc), kc)
        pre = hdot(low, wf_r[:, fcols]) + fb_r[:, fcols]
        R.PRE[...] = pre
        decay = (jnp.minimum(pre, 0.0) - jnp.log1p(jnp.exp(-jnp.abs(pre)))) / normalizer
        for level in range(nl):
            ones = jnp.where(span(level, iota(0), iota(1)), 1.0, 0.0).astype(f32)
            R.XS[level] = jnp.exp(hdot(ones, decay))
        total_decay = jnp.exp(jnp.sum(decay, axis=0, keepdims=True))
        R.DEC[...] = jnp.broadcast_to(total_decay, (8, DK))
        g_end(0)
        R.QKVO[...] = product(normed, R.WA[...])
        keys = R.QKVO[:, kc : 2 * kc]
        values = R.QKVO[:, 2 * kc : 2 * kc + vc]
        R.ST[...] = hdot_rows(values, keys * R.XS[nl - 1]).astype(bf16)

        def seq_pair(sems, src, dst, k, to):
            return remote(src, dst, sems.at[0, k], sems.at[1, k], {SEQ: to})

        for k in range(1, n):
            to = lax.rem(me + k, n)
            copy = seq_pair(S.dec, R.DEC, R.DECL.at[me], k, to)
            copy.start()
            late.append(copy.wait_send)
            ok = me + k < n
            pl.when(ok)(lambda k=k: seq_pair(S.st, R.ST, R.STL.at[me], k, me + k).start())
            guarded(ok, lambda k=k: seq_pair(S.st, R.ST, R.STL.at[me], k, me + k).wait_send())
        d_own(4)
        d_own(5)

        queries = R.QKVO[:, 0:kc] * scale
        i, j = iota(0), iota(1)
        scores = jnp.where(i == j, jnp.sum(queries * keys, axis=-1, keepdims=True), 0.0)
        for level in range(nl - 2):
            xs = R.XS[level]
            up = upper_rows(level)
            part = hdot_t(jnp.where(up, queries * xs, 0.0), jnp.where(up, 0.0, keys * xs))
            scores = jnp.where(mask_of(level), part, scores)
        R.AM[...] = scores
        inside = hdot(scores, values)
        split(R.XN[...], R.XN2, R.XNO)
        split(R.COT[...].astype(bf16), R.GO2, R.GOO)
        act_send(0, R.XNO, R.XN2.at[low_rows])
        act_send(1, R.GOO, R.GO2.at[low_rows])
        d_take(2, 1)
        d_take(2, 2)
        d_take(3, 2)

        for k in range(1, n):
            came = lax.rem(me + n - k, n)
            seq_pair(S.dec, R.DECL.at[came], R.DECL.at[came], k, came).wait_recv()
        R.S0[...] = jnp.zeros((vc, DK), f32)
        for k in range(n - 1, 0, -1):

            @pl.when(me - k >= 0)
            def _():
                src = me - k
                seq_pair(S.st, R.STL.at[src], R.STL.at[src], k, src).wait_recv()
                R.S0[...] = R.DECL[src, 0:1, :] * R.S0[...] + R.STL[src].astype(f32)

        out = hdot_t(queries * R.XS[nl - 2], R.S0[...]) + inside
        R.O[...] = out
        gate = R.QKVO[:, 2 * kc + vc : acols]
        sig3 = lax.logistic(gate)
        scale_three = lax.rsqrt(jnp.mean(out * out, axis=-1, keepdims=True) + epsilon)
        mixed = (out * scale_three * gg_r[...] * (gate * sig3)).astype(bf16)
        R.ZZ[0:tok] = mixed
        d_take(2, 3)
        g_end(2)
        ar_fill(0, product(mixed, R.WO[...]))
        ar_start(0)
        act_send(2, R.ZZ.at[top], R.ZZ.at[low_rows])
        d_take(3, 1)
        ar_mid(0)
        d_take(4, 2)
        ar_end(0)
        hres = R.X[...] + ar_value(0)
        R.HRES[...] = hres
        scale_two = lax.rsqrt(jnp.mean(hres * hres, axis=-1, keepdims=True) + epsilon)
        gain_second = R.SIDE[rank + 1 : rank + 2].astype(f32)
        hn = (hres * scale_two * gain_second).astype(bf16)
        R.HN[...] = hn
        split(hn, R.HN2, R.HNO)
        act_send(3, R.HNO, R.HN2.at[low_rows])
        d_take(5, 2)
        d_take(4, 1)
        d_take(3, 3)
        d_take(5, 1)
        d_take(4, 3)
        g_end(3)
        g_end(4)
        a1 = dot_t(R.HN[...], R.WG[...])
        a2 = dot_t(R.HN[...], R.WU[...])
        d_take(5, 3)
        g_end(5)
        d_hid = dot_t(R.COT[...].astype(bf16), R.WD[...])
        s1 = lax.logistic(a1)
        silu = a1 * s1
        R.MM[0:tok] = (silu * a2).astype(bf16)
        R.DA1[0:tok] = (d_hid * a2 * s1 * (1.0 + a1 * (1.0 - s1))).astype(bf16)
        R.DA2[0:tok] = (d_hid * silu).astype(bf16)
        ar_fill(1, product(R.DA1[0:tok], R.WG[...]) + product(R.DA2[0:tok], R.WU[...]))
        ar_start(1)
        act_send(4, R.DA1.at[top], R.DA1.at[low_rows])
        act_send(5, R.DA2.at[top], R.DA2.at[low_rows])
        act_send(6, R.MM.at[top], R.MM.at[low_rows])
        ar_fill(2, product(R.MM[0:tok], R.WD[...]))
        act_wait(1, R.GOO, R.GO2.at[low_rows])
        act_wait(3, R.HNO, R.HN2.at[low_rows])
        act_wait(4, R.DA1.at[top], R.DA1.at[low_rows])
        R.RG[...] = dot_rows(R.DA1[...], R.HN2[...]).astype(bf16)
        r_start(0, 0)
        r_start(0, 1)
        ar_mid(1)
        ar_start(2)
        act_wait(5, R.DA2.at[top], R.DA2.at[low_rows])
        R.RU[...] = dot_rows(R.DA2[...], R.HN2[...]).astype(bf16)
        r_start(1, 0)
        act_wait(6, R.MM.at[top], R.MM.at[low_rows])
        R.RD[...] = dot_rows(R.MM[...], R.GO2[...]).astype(bf16)
        r_start(2, 0)
        ar_end(1)

        d_hn = ar_value(1)
        hres = R.HRES[...]
        scale_two = lax.rsqrt(jnp.mean(hres * hres, axis=-1, keepdims=True) + epsilon)
        terms, d_norm = norm_back(hres, scale_two, gain_second, d_hn)
        gain_two_grad = jnp.sum(terms, axis=0, keepdims=True)
        d_res = R.COT[...] + d_norm
        R.DRES[...] = d_res
        dy = d_res.astype(bf16)
        d_mixed = dot_t(dy, R.WO[...])
        ar_mid(2)
        out = R.O[...]
        gate = R.QKVO[:, 2 * kc + vc : acols]
        sig3 = lax.logistic(gate)
        scale_three = lax.rsqrt(jnp.mean(out * out, axis=-1, keepdims=True) + epsilon)
        normed_out = out * scale_three * gg_r[...]
        d_on = d_mixed * (gate * sig3)
        d_gate = d_mixed * normed_out * sig3 * (1.0 + gate * (1.0 - sig3))
        R.DP[0:tok, 2 * kc + vc : acols] = d_gate.astype(bf16)
        group_terms, d_out = norm_back(out, scale_three, gg_r[...], d_on)
        group_row = jnp.sum(group_terms, axis=0, keepdims=True)
        queries = R.QKVO[:, 0:kc] * scale
        keys = R.QKVO[:, kc : 2 * kc]
        values = R.QKVO[:, 2 * kc : 2 * kc + vc]
        R.DMIX[...] = d_out
        R.SG[...] = hdot_rows(d_out, queries * R.XS[nl - 2]).astype(bf16)
        for k in range(1, n):
            ok = me - k >= 0
            pl.when(ok)(lambda k=k: seq_pair(S.sg, R.SG, R.SGL.at[me], k, me - k).start())
            guarded(ok, lambda k=k: seq_pair(S.sg, R.SG, R.SGL.at[me], k, me - k).wait_send())
        r_start(1, 1)
        r_start(2, 1)
        split(dy, R.DY2, R.DYO)
        act_send(7, R.DYO, R.DY2.at[low_rows])

        d_out = R.DMIX[...]
        d_scores = hdot_t(d_out, values)
        i, j = iota(0), iota(1)
        diag = jnp.sum(jnp.where(i == j, d_scores, 0.0), axis=-1, keepdims=True)
        d_q = diag * keys
        d_k = diag * queries
        for level in range(nl - 2):
            xs = R.XS[level]
            up = upper_rows(level)
            part = jnp.where(mask_of(level), d_scores, 0.0)
            q_part = xs * hdot(part, jnp.where(up, 0.0, keys * xs))
            k_part = xs * hdot_rows(part, jnp.where(up, queries * xs, 0.0))
            R.GS[level * tok : (level + 1) * tok] = queries * q_part + keys * k_part
            d_q = d_q + q_part
            d_k = d_k + k_part
        q_part = R.XS[nl - 2] * hdot(d_out, R.S0[...])
        R.GS[(nl - 2) * tok : (nl - 1) * tok] = queries * q_part
        d_q = (d_q + q_part) * scale
        R.DP[0:tok, 0:kc] = d_q.astype(bf16)
        d_v = hdot_rows(R.AM[...], d_out)
        r_relay(0)
        R.LG[...] = jnp.zeros((vc, DK), f32)
        for k in range(n - 1, 0, -1):

            @pl.when(me + k < n)
            def _():
                src = me + k
                seq_pair(S.sg, R.SGL.at[src], R.SGL.at[src], k, src).wait_recv()
                R.LG[...] = R.DECL[src, 0:1, :] * R.LG[...] + R.SGL[src].astype(f32)

        later = R.LG[...]
        k_part = R.XS[nl - 1] * hdot(values, later)
        R.GS[(nl - 1) * tok : nl * tok] = keys * k_part
        R.DP[0:tok, kc : 2 * kc] = (d_k + k_part).astype(bf16)
        d_v = d_v + hdot_t(keys * R.XS[nl - 1], later)
        R.DP[0:tok, 2 * kc : 2 * kc + vc] = d_v.astype(bf16)
        act_send(8, R.DP.at[top], R.DP.at[low_rows])
        whole_row = R.DEC[0:1] * jnp.sum(R.S0[...] * later, axis=0, keepdims=True)
        d_decay = jnp.broadcast_to(whole_row, (tok, DK))
        for level in range(nl):
            ones = jnp.where(span(level, iota(1), iota(0)), 1.0, 0.0).astype(f32)
            d_decay = d_decay + hdot(ones, R.GS[level * tok : (level + 1) * tok])
        d_pre = d_decay / normalizer * lax.logistic(-R.PRE[...])
        src3 = R.AST3
        src3[:, :, width:] = jnp.zeros((nh, qrows, 128), bf16)
        d_low_part = hdot_t(d_pre, wf_r[:, fcols]).astype(bf16)
        for k in range(nh):
            src3[k, :, width : width + rank] = d_low_part[k * qrows : (k + 1) * qrows]
        ar_fill(3, dot_t(R.DP[0:tok], R.WA[...]))
        ar_start(3)
        R.SMALL[...] = jnp.zeros((mrows, kc), f32)
        R.SMALL[0:rank] = hdot_rows(R.LOW[...], d_pre)
        R.SMALL[rank : rank + 1] = jnp.sum(d_pre, axis=0, keepdims=True)
        for k in range(grow):
            R.SMALL[rank + 1 + k : rank + 2 + k] = group_row[:, k * kc : (k + 1) * kc]

        def all_pair(sems, src, dst, k, peer):
            return remote(
                src, dst, sems.at[0, k], sems.at[1, k], {SEQ: peer // nd, DP: lax.rem(peer, nd)}
            )

        for k in range(1, n * nd):
            peer = lax.rem(flat + k, n * nd)
            copy = all_pair(S.small, R.SMALL, R.SMALLL.at[flat], k, peer)
            copy.start()
            late.append(copy.wait_send)

        r_relay(1)
        act_wait(7, R.DYO, R.DY2.at[low_rows])
        act_wait(2, R.ZZ.at[top], R.ZZ.at[low_rows])
        R.RO[...] = dot_rows(R.ZZ[...], R.DY2[...]).astype(bf16)
        act_wait(0, R.XNO, R.XN2.at[low_rows])
        act_wait(8, R.DP.at[top], R.DP.at[low_rows])
        R.RA[...] = dot_rows(R.XN2[...], R.DP[...]).astype(bf16)
        for p in (3, 4):
            r_start(p, 0)
            r_start(p, 1)
        ar_mid(3)
        r_relay(2)
        ar_end(2)
        R.BOUT[...] = R.HRES[...] + ar_value(2)
        put_local(8, R.BOUT, bout_h)
        small = R.SMALL[...]
        for k in range(1, n * nd):
            came = lax.rem(flat + n * nd - k, n * nd)
            all_pair(S.small, R.SMALLL.at[came], R.SMALLL.at[came], k, came).wait_recv()
            small = small + R.SMALLL[came]
        R.SMH[...] = small
        R.SMHL[hh] = small
        for k in range(1, nh):
            to = lax.rem(hh + k, nh)
            copy = remote(R.SMH, R.SMHL.at[hh], S.smh.at[0, k], S.smh.at[1, k], {HEAD: to})
            copy.start()
            late.append(copy.wait_send)
        ar_end(3)
        x = R.X[...]
        scale_one = lax.rsqrt(jnp.mean(x * x, axis=-1, keepdims=True) + epsilon)
        gain_first = R.SIDE[rank : rank + 1].astype(f32)
        d_low = jnp.concatenate([R.ASM3[k, :, width : width + rank] for k in range(nh)], axis=0)
        d_xn = ar_value(3) + product(d_low, R.SIDE[0:rank])
        terms, d_norm = norm_back(x, scale_one, gain_first, d_xn)
        gain_one_grad = jnp.sum(terms, axis=0, keepdims=True)
        R.GIN[...] = R.DRES[...] + d_norm
        put_local(9, R.GIN, gin_h)
        low_grad = dot_rows(d_low, R.XN[...])
        R.TALL[...] = jnp.zeros((n, trows, shard), f32)
        for z in range(n):
            cols = slice(z * shard, (z + 1) * shard)
            R.TALL[z, 0:rank] = low_grad[:, cols]
            R.TALL[z, rank : rank + 1] = gain_one_grad[:, cols]
            R.TALL[z, rank + 1 : rank + 2] = gain_two_grad[:, cols]
        for k in range(1, n * nd):
            peer = lax.rem(flat + k, n * nd)
            copy = all_pair(S.tall, R.TALL.at[peer // nd], R.TALLL.at[flat], k, peer)
            copy.start()
            late.append(copy.wait_send)
        for p in range(3):
            r_close(p)
            put(p)
        r_relay(3)
        r_relay(4)
        tall = R.TALL[me]
        for k in range(1, n * nd):
            came = lax.rem(flat + n * nd - k, n * nd)
            all_pair(S.tall, R.TALLL.at[came], R.TALLL.at[came], k, came).wait_recv()
            tall = tall + R.TALLL[came]
        low_o[...] = tall[0:rank]
        again_o[...] = tall[rank : rank + 1]
        mgain_o[...] = tall[rank + 1 : rank + 2]
        for k in range(1, nh):
            came = lax.rem(hh + nh - k, nh)
            remote(R.SMHL.at[came], R.SMHL.at[came], S.smh.at[0, k], S.smh.at[1, k], {HEAD: came}).wait_recv()
        group = jnp.zeros((1, vc), f32)
        for h in range(nh):
            forget_o[:, h * kc : (h + 1) * kc] = R.SMHL[h, 0:rank]
            bias_o[:, h * kc : (h + 1) * kc] = R.SMHL[h, rank : rank + 1]
            group = group + jnp.concatenate(
                [R.SMHL[h, rank + 1 + k : rank + 2 + k] for k in range(grow)], axis=1
            )
        group_o[...] = group
        r_close(3)
        put(3)
        r_close(4)
        for i in range(4, 8):
            put(i)
        for wait in late:
            wait()

    return pl.pallas_call(
        kernel,
        out_shape=out_shape,
        in_specs=in_specs,
        out_specs=out_specs,
        scratch_shapes=scratch,
        compiler_params=pltpu.CompilerParams(
            collective_id=0, has_side_effects=True, vmem_limit_bytes=60 * 2**20
        ),
        name="fused_layer",
    )(*args)


def hand_over(arrays):
    count = len(arrays)

    def kernel(*refs):
        ins, outs, held = refs[:count], refs[count : 2 * count], refs[2 * count : 3 * count]
        sems = refs[3 * count]
        taken = [pltpu.make_async_copy(a, b, sems.at[0, i]) for i, (a, b) in enumerate(zip(ins, held))]
        given = [pltpu.make_async_copy(a, b, sems.at[1, i]) for i, (a, b) in enumerate(zip(held, outs))]
        for copy in taken:
            copy.start()
        for first, second in zip(taken, given):
            first.wait()
            second.start()
        for copy in given:
            copy.wait()

    anys = pl.BlockSpec(memory_space=pl.ANY)
    return pl.pallas_call(
        kernel,
        out_shape=[jax.ShapeDtypeStruct(a.shape, a.dtype) for a in arrays],
        in_specs=[anys] * count,
        out_specs=[anys] * count,
        scratch_shapes=[pltpu.VMEM(a.shape, a.dtype) for a in arrays] + [pltpu.SemaphoreType.DMA((2, count))],
        compiler_params=pltpu.CompilerParams(vmem_limit_bytes=60 * 2**20),
        name="hand_over",
    )(*arrays)


def one_kernel(
    x_in, cotangent, attn_gain, w_query, w_key, w_value, w_outgate, w_lowrank, w_forget, forget_bias,
    group_gain, w_output, mlp_gain, w_gate, w_up, w_down,
):
    n, nh, nd = lax.axis_size("seq"), lax.axis_size("head"), lax.axis_size("dp")
    _, tok, width = x_in.shape
    shard, rank = w_lowrank.shape
    kc, vc, hid = w_query.shape[1], w_value.shape[1], w_gate.shape[1]
    side = jnp.concatenate(
        (w_lowrank.T, attn_gain[None, :], mlp_gain[None, :], jnp.zeros((rank - 2, shard), jnp.bfloat16)), axis=0
    )
    outs = fused_layer(
        (n, nh, nd),
        (tok, width, shard, kc, vc, hid, rank),
        (
            x_in.reshape(tok, width),
            cotangent.reshape(tok, width),
            side,
            w_query,
            w_key,
            w_value,
            w_outgate,
            w_forget,
            forget_bias[None, :],
            group_gain[None, :],
            w_output,
            w_gate.T,
            w_up.T,
            w_down,
        ),
    )
    (result, grad_in, gq, gk, gv, gog, gwo, gg, gu, gd, glow, gain1, gain2, gforget, gbias, ggroup) = hand_over(outs)
    return (
        result[None],
        grad_in[None],
        gain1[0],
        gq,
        gk,
        gv,
        gog,
        glow.T,
        gforget,
        gbias[0],
        ggroup[0],
        gwo,
        gain2[0],
        gg.T,
        gu.T,
        gd,
    )


def fits_one_kernel(x_in, w_query, w_lowrank, w_value, w_gate):
    seqs, tok, _ = x_in.shape
    shard, rank = w_lowrank.shape
    n_head, n_dp = lax.axis_size("head"), lax.axis_size("dp")
    return (
        seqs == 1
        and n_dp == 2
        and lax.axis_size("seq") in (2, 3, 4)
        and tok & (tok - 1) == 0
        and tok % (16 * n_head) == 0
        and shard % 256 == 0
        and w_query.shape[1] == DK
        and w_value.shape[1] == DV
        and w_gate.shape[1] % 32 == 0
        and rank % 16 == 0
    )


def per_device(*args):
    x_in, w_query, w_value, w_lowrank, w_gate = args[0], args[3], args[5], args[7], args[13]
    if fits_one_kernel(x_in, w_query, w_lowrank, w_value, w_gate):
        return one_kernel(*args)
    return on_device(*args)


def solution(mesh):
    return jax.shard_map(
        per_device,
        mesh=mesh,
        in_specs=(
            P("dp", "seq", None),
            P("dp", "seq", None),
            P("seq"),
            P("seq", "head"),
            P("seq", "head"),
            P("seq", "head"),
            P("seq", "head"),
            P("seq", None),
            P(),
            P(),
            P(),
            P("head", "seq"),
            P("seq"),
            P("seq", "head"),
            P("seq", "head"),
            P("head", "seq"),
        ),
        out_specs=(
            P("dp", "seq", None),
            P("dp", "seq", None),
            P("seq"),
            P("seq", "head"),
            P("seq", "head"),
            P("seq", "head"),
            P("seq", "head"),
            P("seq", None),
            P(),
            P(),
            P(),
            P("head", "seq"),
            P("seq"),
            P("seq", "head"),
            P("seq", "head"),
            P("head", "seq"),
        ),
        check_vma=False,
    )
```
